32 devices in a mesh: mem: 2 (over core), tile: 16 (over z, y, x).
Axes of the slice: x: 2, y: 2, z: 4, core: 2. Of those that a mesh axis runs over, the one named last changes fastest.
Arguments:
- ensemble: bfloat16 [512, 65536], P('mem', 'tile'), may hold values from -6 to 6
- predicted: bfloat16 [512, 65536], P('mem', 'tile'), may hold values from -6 to 6
- obs_noise: bfloat16 [512, 65536], P('mem', 'tile'), may hold values from -6 to 6
- observed: float32 [65536], P('tile'), may hold values from -24 to 24
- noise_var: float32 [65536], P('tile'), may hold values from 32 to 128
- block_lists: int32 [32, 64], replicated, may hold values from 0 to 511, as said below
- taper_weights: float32 [32, 64], replicated, may hold values from 0.05 to 1
Outputs:
- analysis: bfloat16 [512, 65536], P('mem', 'tile')
The draws below stay inside these ranges and needn't reach their ends.
Inputs may be any that keep to these rules, and one draw needn't show every extreme that they name: `block_lists`: each row names 64 distinct blocks, all held by tile indices within 1 of the tile's own index t // 2, counted around the axis.
All inputs are finite; a program needn't handle non-finite values.
Results may differ from the reference program's by a relative error of at most 0.007.
Values may be sent and summed in bfloat16 or wider, within the bound.
No kernel may reach another device: no remote copies, remote signals or barrier semaphores. Data moves between devices by JAX's collectives and lax.ppermute only.
A program may use at most 128 MiB of HBM per device.

```python
import math
import jax
import jax.numpy as jnp
from jax import lax

MEMBERS = 512
BLOCK_ROWS = 128
B_DEV = 32
TPD = 2
TILE_CELLS = 2048
BLOCKS = 512
OBS = 65536
TILES = 32
CELLS = 65536
LIST = 64
N_TILE = 16


def draw_block_lists(key, part):
    reach_dev = max(1, N_TILE // 16)
    window = (2 * reach_dev + 1) * B_DEV
    subkeys = jax.random.split(jax.random.fold_in(key, 17), TILES)
    chosen = jax.vmap(lambda single: jax.random.permutation(single, window))(subkeys)[:, :LIST]
    owners = jnp.arange(TILES, dtype=jnp.int32) // TPD
    offset = (owners - reach_dev) * B_DEV
    return ((offset[:, None] + chosen.astype(jnp.int32)) % BLOCKS).astype(jnp.int32)


def draw_predicted(key, part):
    mode_count = 16
    subkeys = jax.random.split(jax.random.fold_in(key, 29), 5)
    independent = jax.random.normal(subkeys[0], (MEMBERS, OBS), jnp.float32)
    amplitude = jnp.exp(jax.random.uniform(subkeys[1], (mode_count,), jnp.float32, math.log(0.1), math.log(0.6)))
    row_scale = jnp.exp(jax.random.uniform(subkeys[2], (MEMBERS, 1), jnp.float32, math.log(0.5), math.log(1.5)))
    loadings = jax.random.normal(subkeys[3], (MEMBERS, mode_count), jnp.float32)
    patterns = jax.random.normal(subkeys[4], (mode_count, OBS), jnp.float32)
    sample_field = independent * row_scale
    for number in range(mode_count):
        sample_field = sample_field + amplitude[number] * loadings[:, number:number + 1] * patterns[number:number + 1, :]
    return jnp.clip(sample_field, -6.0, 6.0).astype(jnp.bfloat16)


def level_of(rng, extent, pieces, least, top_value):
    def one(dim, parts):
        heights = jax.random.uniform(jax.random.fold_in(jax.random.fold_in(rng, 6), dim), (parts,), jnp.float32, least / len(pieces), top_value / len(pieces))
        return jnp.repeat(jnp.exp(heights), extent[dim] // parts).reshape((-1,) + (1,) * (len(extent) - dim - 1))

    loudness = one(*pieces[0])
    for cut in pieces[1:]:
        loudness = loudness * one(*cut)
    return loudness


def normal_values(rng, extent, deviation, limit, shards=(), kind=jnp.bfloat16):
    drawn = deviation * jax.random.normal(rng, extent, jnp.float32)
    if shards:
        drawn = drawn * level_of(rng, extent, shards, -0.22, 0.18)
    return jnp.clip(drawn, -limit, limit).astype(kind)


def setup_inputs(seed: int = 0) -> dict:
    keys = jax.random.split(jax.random.key(seed), 8)
    return {
        "ensemble": normal_values(keys[0], (MEMBERS, CELLS), 1.0, 6.0, ((0, 2), (1, 16))),
        "predicted": draw_predicted(jax.random.fold_in(keys[7], 71), 0),
        "obs_noise": normal_values(keys[2], (MEMBERS, OBS), 1.0, 6.0, ((0, 2), (1, 16))),
        "observed": normal_values(keys[3], (OBS,), 4.0, 24.0, ((0, 16),), jnp.float32),
        "noise_var": jnp.clip(jnp.exp(math.log(128.0) - 1.3862944 * jax.random.uniform(keys[4], (OBS,), jnp.float32) ** level_of(keys[4], (OBS,), ((0, 16),), -0.2, 0.2)), 32.0, 128.0),
        "block_lists": draw_block_lists(jax.random.fold_in(keys[7], 71), 0),
        "taper_weights": jnp.clip(jnp.exp(jax.random.uniform(keys[6], (TILES, LIST), jnp.float32, math.log(0.05), math.log(1.0))), 0.05, 1.0),
    }


def chol_apply(factor, rhs):
    lower_part = lax.linalg.triangular_solve(factor, rhs, left_side=True, lower=True)
    return lax.linalg.triangular_solve(factor, lower_part, left_side=True, lower=True, transpose_a=True)

def reference(ensemble, predicted, obs_noise, observed, noise_var, block_lists, taper_weights):
    pred_wide = predicted.astype(jnp.float32)
    model_wide = ensemble.astype(jnp.float32)
    data_anom = (pred_wide - lax.optimization_barrier(jnp.sum(pred_wide, axis=0)) / MEMBERS).astype(jnp.bfloat16)
    model_anom = (model_wide - lax.optimization_barrier(jnp.sum(model_wide, axis=0)) / MEMBERS).astype(jnp.bfloat16)
    inverse_var = 1.0 / noise_var
    innovation = observed + jnp.sqrt(noise_var) * obs_noise.astype(jnp.float32) - pred_wide
    weighted = (data_anom.astype(jnp.float32) * inverse_var).astype(jnp.bfloat16)
    prior_diag = (MEMBERS - 1.0) * jnp.eye(MEMBERS, dtype=jnp.float32)
    ens = jnp.dot(data_anom.astype(jnp.float32), weighted.T.astype(jnp.float32), preferred_element_type=jnp.float32) + prior_diag
    pcols = jnp.dot(innovation.astype(jnp.bfloat16).astype(jnp.float32), weighted.T.astype(jnp.float32), preferred_element_type=jnp.float32)
    factor = jnp.linalg.cholesky(ens)
    coeffs = chol_apply(factor, pcols.T).T.astype(jnp.bfloat16)
    correction = jnp.dot(coeffs.astype(jnp.float32), data_anom.astype(jnp.float32), preferred_element_type=jnp.float32)
    vgain = ((innovation - correction) * inverse_var).astype(jnp.bfloat16)
    gain_blocks = vgain.reshape(MEMBERS, BLOCKS, BLOCK_ROWS)
    anom_blocks = data_anom.reshape(MEMBERS, BLOCKS, BLOCK_ROWS)

    def one_tile(index):
        listed = block_lists[index].astype(jnp.int32)
        weights = taper_weights[index]
        chosen_gain = jnp.take(gain_blocks, listed, axis=1).astype(jnp.float32) * weights[None, :, None]
        chosen_anom = jnp.take(anom_blocks, listed, axis=1).astype(jnp.float32)
        total = jnp.einsum('jbo,kbo->jk', chosen_gain, chosen_anom, precision=lax.Precision.HIGHEST)
        gain = (total * (1.0 / (MEMBERS - 1))).astype(jnp.bfloat16)
        start = (index * TILE_CELLS).astype(jnp.int32)
        anom_cells = lax.dynamic_slice_in_dim(model_anom, start, TILE_CELLS, 1)
        prior_cells = lax.dynamic_slice_in_dim(model_wide, start, TILE_CELLS, 1)
        return (prior_cells + jnp.dot(gain.astype(jnp.float32), anom_cells.astype(jnp.float32), preferred_element_type=jnp.float32)).astype(jnp.bfloat16)
    updated = lax.map(one_tile, jnp.arange(TILES, dtype=jnp.int32))
    return jnp.transpose(updated, (1, 0, 2)).reshape(MEMBERS, CELLS)
```

```python
import functools

import jax
import jax.numpy as jnp
from jax import lax
from jax.experimental import pallas as pl
from jax.experimental.pallas import tpu as pltpu
from jax.sharding import PartitionSpec as P

BLOCK_ROWS = 128
TPD = 2
F32 = jnp.float32
BF16 = jnp.bfloat16
VMEM_LIMIT = 48 * 1024 * 1024


def dot_nt(a, b):
    return lax.dot_general(a, b, (((1,), (1,)), ((), ())), preferred_element_type=F32)


def dot_nn(a, b):
    return lax.dot_general(a, b, (((1,), (0,)), ((), ())), preferred_element_type=F32)


def high_low(x):
    high = x.astype(BF16).astype(F32)
    return high, x - high


def pack(ref, base, unit, parts):
    diag, off, left, right = parts
    diag_hi, diag_lo = high_low(diag)
    off_hi, off_lo = high_low(off)
    ref[base:base + unit, :] = diag_hi.astype(BF16)
    ref[base + unit:base + 2 * unit, :] = diag_lo.astype(BF16)
    ref[base + 2 * unit:base + 3 * unit, :] = jnp.concatenate([off_hi, off_lo], 0).astype(BF16)
    ref[base + 3 * unit:base + 4 * unit, :] = left.astype(BF16)
    ref[base + 4 * unit:base + 5 * unit, :] = right.astype(BF16)


def unpack(value, unit):
    wide = value.astype(F32)
    diag = wide[0:unit] + wide[unit:2 * unit]
    off = wide[2 * unit:2 * unit + unit // 2] + wide[2 * unit + unit // 2:3 * unit]
    return diag, off, wide[3 * unit:4 * unit], wide[4 * unit:5 * unit]


def put_wide(ref, base, unit, parts):
    diag, off, left, right = parts
    half_unit = unit // 2
    ref[base:base + unit, :] = diag
    ref[base + unit:base + unit + half_unit, :] = off
    ref[base + unit + half_unit:base + 2 * unit + half_unit, :] = left
    ref[base + 2 * unit + half_unit:base + 3 * unit + half_unit, :] = right


def split_wide(value, unit):
    half_unit = unit // 2
    return (
        value[0:unit],
        value[unit:unit + half_unit],
        value[unit + half_unit:2 * unit + half_unit],
        value[2 * unit + half_unit:3 * unit + half_unit],
    )


def prepare_kernel(half, where, own_pred, rem_pred, noise, observed, noise_var,
                   anom, base, keep, send1, send2, send3, diag_acc, off_acc, prod_acc, scaled):
    step = pl.program_id(0)
    group = where[0]
    own_at = pl.multiple_of(group * half, half)
    rem_at = pl.multiple_of((1 - group) * half, half)
    own = own_pred[...].astype(F32)
    rem = rem_pred[...].astype(F32)
    mean = (jnp.sum(own, 0, keepdims=True) + jnp.sum(rem, 0, keepdims=True)) * (0.5 / half)
    own_anom = (own - mean).astype(BF16)
    rem_anom = (rem - mean).astype(BF16)
    variance = noise_var[...]
    deviation = jnp.sqrt(variance)
    scale = 1.0 / deviation
    own_wide = own_anom.astype(F32)
    anom[pl.ds(own_at, half), :] = own_anom
    anom[pl.ds(rem_at, half), :] = rem_anom
    own_scaled = (own_wide * scale).astype(BF16)
    scaled[pl.ds(own_at, half), :] = own_scaled
    scaled[pl.ds(rem_at, half), :] = (rem_anom.astype(F32) * scale).astype(BF16)
    forcing = observed[...] + deviation * noise[...].astype(F32) - own + own_wide
    base[...] = forcing.astype(BF16)
    quarter_at = pl.multiple_of(group * (half // 2), half // 2)
    diag = dot_nt(own_scaled, own_scaled)
    off = dot_nt(scaled[pl.ds(quarter_at, half // 2), :], scaled[half:2 * half, :])
    prod = dot_nt((forcing * scale).astype(BF16), scaled[...])

    @pl.when(step == 0)
    def _():
        diag_acc[...] = diag
        off_acc[...] = off
        prod_acc[...] = prod

    @pl.when(step != 0)
    def _():
        diag_acc[...] += diag
        off_acc[...] += off
        prod_acc[...] += prod

    @pl.when(step == pl.num_programs(0) - 1)
    def _():
        rows = half // 4
        unit = half // 16
        for k, out in enumerate((keep, send1, send2, send3)):
            digit = jnp.bitwise_xor(where[1], k)
            diag_rows = diag_acc[pl.ds(pl.multiple_of(digit * rows, rows), rows), :]
            off_rows = off_acc[pl.ds(pl.multiple_of(digit * (rows // 2), rows // 2), rows // 2), :]
            prod_rows = prod_acc[pl.ds(pl.multiple_of(digit * rows, rows), rows), :]
            for q in range(4):
                parts = (
                    diag_rows[q * unit:(q + 1) * unit],
                    off_rows[q * (unit // 2):(q + 1) * (unit // 2)],
                    prod_rows[q * unit:(q + 1) * unit, :half],
                    prod_rows[q * unit:(q + 1) * unit, half:],
                )
                if k == 0:
                    put_wide(out, q * (unit * 7 // 2), unit, parts)
                else:
                    pack(out, q * unit * 5, unit, parts)


def prepare(where, own_pred, rem_pred, noise, observed, noise_var):
    half, samples = own_pred.shape
    chunk = min(512, samples)
    unit = half // 16
    column = lambda j: (0, j)
    fixed = lambda j: (0, 0)
    sent = jax.ShapeDtypeStruct((20 * unit, half), BF16)
    sent_spec = pl.BlockSpec((20 * unit, half), fixed)
    return pl.pallas_call(
        functools.partial(prepare_kernel, half),
        grid=(samples // chunk,),
        in_specs=[
            pl.BlockSpec(memory_space=pltpu.SMEM),
            pl.BlockSpec((half, chunk), column),
            pl.BlockSpec((half, chunk), column),
            pl.BlockSpec((half, chunk), column),
            pl.BlockSpec((1, chunk), column),
            pl.BlockSpec((1, chunk), column),
        ],
        out_specs=[
            pl.BlockSpec((2 * half, chunk), column),
            pl.BlockSpec((half, chunk), column),
            pl.BlockSpec((14 * unit, half), fixed),
            sent_spec, sent_spec, sent_spec,
        ],
        out_shape=[
            jax.ShapeDtypeStruct((2 * half, samples), BF16),
            jax.ShapeDtypeStruct((half, samples), BF16),
            jax.ShapeDtypeStruct((14 * unit, half), F32),
            sent, sent, sent,
        ],
        scratch_shapes=[
            pltpu.VMEM((half, half), F32),
            pltpu.VMEM((half // 2, half), F32),
            pltpu.VMEM((half, 2 * half), F32),
            pltpu.VMEM((2 * half, chunk), BF16),
        ],
        compiler_params=pltpu.CompilerParams(vmem_limit_bytes=VMEM_LIMIT),
        cost_estimate=pl.CostEstimate(
            flops=5 * half * half * samples, bytes_accessed=12 * half * samples, transcendentals=0
        ),
        name="prepare",
    )(where, own_pred, rem_pred, noise, observed.reshape(1, -1), noise_var.reshape(1, -1))


def first_sum_kernel(unit, where, keep, got1, got2, got3, own, send1, send2, send3):
    for k, out in enumerate((own, send1, send2, send3)):
        digit = jnp.bitwise_xor(where[2], k)
        wide_rows = unit * 7 // 2
        parts = split_wide(keep[pl.ds(pl.multiple_of(digit * wide_rows, 8), wide_rows), :], unit)
        for got in (got1, got2, got3):
            more = unpack(got[pl.ds(pl.multiple_of(digit * 5 * unit, 16), 5 * unit), :], unit)
            parts = tuple(a + b for a, b in zip(parts, more))
        if k == 0:
            put_wide(out, 0, unit, parts)
        else:
            pack(out, 0, unit, parts)


def next_sum_kernel(unit, keep, got1, got2, got3, total, packed):
    parts = split_wide(keep[...], unit)
    for got in (got1, got2, got3):
        parts = tuple(a + b for a, b in zip(parts, unpack(got[...], unit)))
    put_wide(total, 0, unit, parts)
    pack(packed, 0, unit, parts)


def first_sum(where, keep, got):
    half = keep.shape[1]
    unit = half // 16
    sent = jax.ShapeDtypeStruct((5 * unit, half), BF16)
    return pl.pallas_call(
        functools.partial(first_sum_kernel, unit),
        in_specs=[pl.BlockSpec(memory_space=pltpu.SMEM)] + [pl.BlockSpec(memory_space=pltpu.VMEM)] * 4,
        out_specs=[pl.BlockSpec(memory_space=pltpu.VMEM)] * 4,
        out_shape=[jax.ShapeDtypeStruct((unit * 7 // 2, half), F32), sent, sent, sent],
        name="first_sum",
    )(where, keep, *got)


def next_sum(keep, got):
    half = keep.shape[1]
    unit = half // 16
    return pl.pallas_call(
        functools.partial(next_sum_kernel, unit),
        in_specs=[pl.BlockSpec(memory_space=pltpu.VMEM)] * 4,
        out_specs=[pl.BlockSpec(memory_space=pltpu.VMEM)] * 2,
        out_shape=[
            jax.ShapeDtypeStruct((unit * 7 // 2, half), F32),
            jax.ShapeDtypeStruct((5 * unit, half), BF16),
        ],
        name="next_sum",
    )(keep, *got)


def swap_digit(value, stage):
    count = lax.axis_size("tile")
    return [
        lax.ppermute(value[k - 1], "tile", [(i, i ^ (k << (2 * stage))) for i in range(count)])
        for k in (1, 2, 3)
    ]


def swap_group(value):
    return lax.ppermute(value, "mem", [(0, 1), (1, 0)])


def tile_kernel(half, tiles, where, anom, base, scale, *rest):
    outs, accs = rest[:tiles], rest[tiles:]
    step = pl.program_id(0)
    group = where[0]
    own_at = pl.multiple_of(group * half, half)
    quarter_at = pl.multiple_of(group * (half // 2), half // 2)
    own = anom[pl.ds(own_at, half), :]
    own_wide = own.astype(F32)
    quarter = anom[pl.ds(quarter_at, half // 2), :].astype(F32)
    forcing = base[...].astype(F32)
    second = anom[half:2 * half, :]
    everything = anom[...]
    for t in range(tiles):
        weight = scale[t:t + 1, :]
        diag = dot_nt((own_wide * weight).astype(BF16), own)
        off = dot_nt((quarter * weight).astype(BF16), second)
        prod = dot_nt((forcing * weight).astype(BF16), everything)
        acc = accs[t]

        @pl.when(step == 0)
        def _():
            acc[0:half, :] = diag
            acc[half:half * 3 // 2, :] = off
            acc[half * 3 // 2:half * 5 // 2, :] = prod[:, :half]
            acc[half * 5 // 2:half * 7 // 2, :] = prod[:, half:]

        @pl.when(step != 0)
        def _():
            acc[0:half, :] += diag
            acc[half:half * 3 // 2, :] += off
            acc[half * 3 // 2:half * 5 // 2, :] += prod[:, :half]
            acc[half * 5 // 2:half * 7 // 2, :] += prod[:, half:]

    @pl.when(step == pl.num_programs(0) - 1)
    def _():
        for out, acc in zip(outs, accs):
            out[...] = acc[...].astype(out.dtype)


def tile_terms(where, anom, base, scale, kind):
    half, samples = base.shape
    tiles = scale.shape[0]
    chunk = min(1024, samples)
    column = lambda j: (0, j)
    rows = half * 7 // 2
    return pl.pallas_call(
        functools.partial(tile_kernel, half, tiles),
        grid=(samples // chunk,),
        in_specs=[
            pl.BlockSpec(memory_space=pltpu.SMEM),
            pl.BlockSpec((2 * half, chunk), column),
            pl.BlockSpec((half, chunk), column),
            pl.BlockSpec((tiles, chunk), column),
        ],
        out_specs=[pl.BlockSpec((rows, half), lambda j: (0, 0))] * tiles,
        out_shape=[jax.ShapeDtypeStruct((rows, half), kind)] * tiles,
        scratch_shapes=[pltpu.VMEM((rows, half), F32)] * tiles,
        compiler_params=pltpu.CompilerParams(vmem_limit_bytes=VMEM_LIMIT),
        cost_estimate=pl.CostEstimate(
            flops=7 * half * half * samples * tiles, bytes_accessed=6 * half * samples, transcendentals=0
        ),
        name="tile_terms",
    )(where, anom, base, scale)


def solve_kernel(half, where, *refs):
    own_refs, rem_refs, out = refs[0:4], refs[4:8], refs[8]
    matrix, right, own_diag, rem_diag, own_off, rem_off = refs[9:]
    group = where[0]
    unit = half // 16
    members = 2 * half
    prior = members - 1.0
    for kp in range(4):
        for kq in range(4):
            digit = jnp.bitwise_xor(where[1], kp) * 4 + jnp.bitwise_xor(where[2], kq)
            diag_at = pl.ds(pl.multiple_of(digit * unit, unit), unit)
            off_at = pl.ds(pl.multiple_of(digit * (unit // 2), unit // 2), unit // 2)
            part = slice(kq * 5 * unit, (kq + 1) * 5 * unit)
            diag, off, left, rest = unpack(own_refs[kp][part, :], unit)
            own_diag[diag_at, :] = diag
            own_off[off_at, :] = off
            right[diag_at, 0:half] = left
            right[diag_at, half:members] = rest
            diag, off, _, _ = unpack(rem_refs[kp][part, :], unit)
            rem_diag[diag_at, :] = diag
            rem_off[off_at, :] = off
    first = group == 0
    off = jnp.concatenate(
        [jnp.where(first, own_off[...], rem_off[...]), jnp.where(first, rem_off[...], own_off[...])], 0
    )
    row_at = lax.broadcasted_iota(jnp.int32, (half, half), 0)
    col_at = lax.broadcasted_iota(jnp.int32, (half, half), 1)
    eye = jnp.where(row_at == col_at, prior, 0.0)
    matrix[0:half, 0:half] = jnp.where(first, own_diag[...], rem_diag[...]) + eye
    matrix[half:members, half:members] = jnp.where(first, rem_diag[...], own_diag[...]) + eye
    matrix[0:half, half:members] = off
    matrix[half:members, 0:half] = off.T
    right[:, 0:half] += jnp.where(first, eye, 0.0)
    right[:, half:members] += jnp.where(first, 0.0, eye)

    whole = matrix[...]
    row_bound = jnp.max(jnp.sum(jnp.abs(whole), axis=1))
    top = jnp.minimum(row_bound, jnp.sqrt(jnp.sum(whole * whole))) * 1.0001
    factor = 2.0 / (top + prior)
    matrix[...] = whole * factor
    right[...] = right[...] * factor

    def update(spread):
        y = matrix[...]
        y_hi = y.astype(BF16)
        y_lo = (y - y_hi.astype(F32)).astype(BF16)
        c = right[...]
        c_hi = c.astype(BF16)
        c_lo = (c - c_hi.astype(F32)).astype(BF16)
        square = spread * spread
        s = 2.0 / (2.0 - square)
        matrix[...] = s * (2.0 * y - (dot_nn(y_hi, y_hi) + dot_nn(y_hi, y_lo) + dot_nn(y_lo, y_hi)))
        right[...] = s * (2.0 * c - (dot_nn(c_hi, y_hi) + dot_nn(c_hi, y_lo) + dot_nn(c_lo, y_hi)))
        return square / (2.0 - square)

    lax.while_loop(lambda spread: spread > 0.02, update, (top - prior) / (top + prior))
    y = matrix[...]
    y_hi = y.astype(BF16)
    y_lo = (y - y_hi.astype(F32)).astype(BF16)
    c = right[...]
    c_hi = c.astype(BF16)
    c_lo = (c - c_hi.astype(F32)).astype(BF16)
    last = 2.0 * c - (dot_nn(c_hi, y_hi) + dot_nn(c_hi, y_lo) + dot_nn(c_lo, y_hi))
    out[...] = last.astype(BF16)


def solve(where, own, rem):
    half = own[0].shape[1]
    return pl.pallas_call(
        functools.partial(solve_kernel, half),
        in_specs=[pl.BlockSpec(memory_space=pltpu.SMEM)] + [pl.BlockSpec(memory_space=pltpu.VMEM)] * 8,
        out_specs=pl.BlockSpec(memory_space=pltpu.VMEM),
        out_shape=jax.ShapeDtypeStruct((half, 2 * half), BF16),
        scratch_shapes=[
            pltpu.VMEM((2 * half, 2 * half), F32),
            pltpu.VMEM((half, 2 * half), F32),
            pltpu.VMEM((half, half), F32),
            pltpu.VMEM((half, half), F32),
            pltpu.VMEM((half // 2, half), F32),
            pltpu.VMEM((half // 2, half), F32),
        ],
        compiler_params=pltpu.CompilerParams(vmem_limit_bytes=VMEM_LIMIT),
        cost_estimate=pl.CostEstimate(
            flops=8 * 10 * half**3 * 3, bytes_accessed=16 * half * half, transcendentals=0
        ),
        name="solve",
    )(where, *own, *rem)


def finish_kernel(half, arrivals, where, coeffs, own_sum, rem_sum, own_prod, *rest):
    got = rest[:arrivals]
    own_model, rem_model, out, own_gain, rem_gain = rest[arrivals:]
    first = where[0] == 0

    @pl.when(pl.program_id(1) == 0)
    def _():
        own = own_sum[0]
        rem = rem_sum[0]
        top = jnp.where(first, own[0:half], rem[0:half])
        low = jnp.where(first, rem[0:half], own[0:half])
        off = jnp.concatenate(
            [
                jnp.where(first, own[half:], rem[half:]),
                jnp.where(first, rem[half:], own[half:]),
            ],
            0,
        )
        left_c = coeffs[:, 0:half]
        right_c = coeffs[:, half:2 * half]
        prod = own_prod[0, half * 3 // 2:, :]
        for piece in got:
            prod = prod + piece[0, half * 3 // 2:, :].astype(F32)
        scale = 1.0 / (2.0 * half - 1.0)
        left = (prod[0:half] - (dot_nn(left_c, top) + dot_nt(right_c, off))) * scale
        right = (prod[half:] - (dot_nn(left_c, off) + dot_nn(right_c, low))) * scale
        mean = (jnp.sum(left, 1, keepdims=True) + jnp.sum(right, 1, keepdims=True)) * (0.5 / half)
        left = (left - mean).astype(BF16)
        right = (right - mean).astype(BF16)
        own_gain[...] = jnp.where(first, left, right)
        rem_gain[...] = jnp.where(first, right, left)

    own = own_model[...]
    update = dot_nn(own_gain[...], own) + dot_nn(rem_gain[...], rem_model[...])
    out[...] = (own.astype(F32) + update).astype(BF16)


def finish(where, coeffs, own_sum, rem_sum, own_prod, got, own_model, rem_model):
    half, cells = own_model.shape
    chunk = min(1024, cells // TPD)
    steps = cells // TPD // chunk
    column = lambda t, j: (0, t * steps + j)
    tile = lambda t, j: (t, 0, 0)
    rows = half * 7 // 2
    return pl.pallas_call(
        functools.partial(finish_kernel, half, len(got)),
        grid=(TPD, steps),
        in_specs=[
            pl.BlockSpec(memory_space=pltpu.SMEM),
            pl.BlockSpec((half, 2 * half), lambda t, j: (0, 0)),
            pl.BlockSpec((1, half * 3 // 2, half), tile),
            pl.BlockSpec((1, half * 3 // 2, half), tile),
        ]
        + [pl.BlockSpec((1, rows, half), tile)] * (1 + len(got))
        + [pl.BlockSpec((half, chunk), column)] * 2,
        out_specs=pl.BlockSpec((half, chunk), column),
        out_shape=jax.ShapeDtypeStruct((half, cells), BF16),
        scratch_shapes=[pltpu.VMEM((half, half), BF16)] * 2,
        compiler_params=pltpu.CompilerParams(vmem_limit_bytes=VMEM_LIMIT),
        cost_estimate=pl.CostEstimate(
            flops=4 * half * half * cells, bytes_accessed=6 * half * cells, transcendentals=0
        ),
        name="finish",
    )(where, coeffs, own_sum, rem_sum, own_prod, *got, own_model, rem_model)


def sample_weights(block_lists, taper_weights, targets, source, inverse_var):
    blocks_local = inverse_var.shape[0] // BLOCK_ROWS
    rows = [lax.dynamic_slice_in_dim(block_lists, target * TPD, TPD, 0) for target in targets]
    tapers = [lax.dynamic_slice_in_dim(taper_weights, target * TPD, TPD, 0) for target in targets]
    rows, tapers = jnp.concatenate(rows, 0), jnp.concatenate(tapers, 0)
    ids = source * blocks_local + jnp.arange(blocks_local, dtype=jnp.int32)
    matches = rows[:, None, :] == ids[None, :, None]
    weights = jnp.sum(jnp.where(matches, tapers[:, None, :], 0.0), axis=2)
    scaled = weights[:, :, None] * inverse_var.reshape(1, blocks_local, BLOCK_ROWS)
    return scaled.reshape(rows.shape[0], -1)


def shards(ensemble, predicted, obs_noise, observed, noise_var, block_lists, taper_weights):
    half = predicted.shape[0]
    count = lax.axis_size("tile")
    index = lax.axis_index("tile")
    where = jnp.stack([lax.axis_index("mem"), index % 4, (index // 4) % 4]).astype(jnp.int32)
    rem_pred = swap_group(predicted)
    rem_model = swap_group(ensemble)

    reach = max(1, count // 16)
    relay = reach == 1
    if relay:
        partner = index + 1 - 2 * (index % 2)
        far = (index - 1 + 2 * (index % 2)) % count
        targets = [far, partner, index]
    else:
        offsets = [o for o in range(-reach, reach + 1) if o != 0]
        targets = [(index + o) % count for o in offsets] + [index]
    scales = sample_weights(block_lists, taper_weights, targets, index, 1.0 / noise_var)

    anom, base, keep, *send = prepare(where, predicted, rem_pred, obs_noise, observed, noise_var)

    got = swap_digit(send, 0)
    keep, *send = first_sum(where, keep, got)
    got = swap_digit(send, 1)
    keep, packed = next_sum(keep, got)
    stage = 2
    while 4**stage < count:
        keep, packed = next_sum(keep, swap_digit([packed] * 3, stage))
        stage += 1
    whole = jnp.concatenate([packed] + swap_digit([packed] * 3, 1), 0)
    own = [whole] + swap_digit([whole] * 3, 0)
    rem = [swap_group(piece) for piece in own]

    if relay:
        sent = tile_terms(where, anom, base, scales[0:TPD], BF16)
        hop = [(i, (i + 2) % count if i % 2 else (i - 2) % count) for i in range(count)]
        passed = [lax.ppermute(piece, "tile", hop) for piece in sent]
        near = tile_terms(where, anom, base, scales[TPD:2 * TPD], F32)
        pair = [(i, i ^ 1) for i in range(count)]
        arrived = [
            lax.ppermute((a + b.astype(F32)).astype(BF16), "tile", pair) for a, b in zip(near, passed)
        ]
        arrivals = [jnp.stack(arrived)]
    else:
        arrivals = []
        for n, offset in enumerate(offsets):
            terms = tile_terms(where, anom, base, scales[n * TPD:(n + 1) * TPD], BF16)
            by = [(i, (i + offset) % count) for i in range(count)]
            arrivals.append(lax.ppermute(jnp.stack(terms), "tile", by))
    own_terms = jnp.stack(tile_terms(where, anom, base, scales[-TPD:], F32))
    own_sum = own_terms[:, :half * 3 // 2]
    for piece in arrivals:
        own_sum = own_sum + piece[:, :half * 3 // 2].astype(F32)
    own_sum = own_sum.astype(BF16)
    rem_sum = swap_group(own_sum)

    coeffs = solve(where, own, rem)
    return finish(where, coeffs, own_sum, rem_sum, own_terms, arrivals, ensemble, rem_model)


def solution(mesh):
    in_specs = (
        P("mem", "tile"),
        P("mem", "tile"),
        P("mem", "tile"),
        P("tile"),
        P("tile"),
        P(),
        P(),
    )
    out_specs = P("mem", "tile")
    return jax.shard_map(shards, mesh=mesh, in_specs=in_specs, out_specs=out_specs, check_vma=False)
```

```python
import functools

import jax
import jax.numpy as jnp
from jax import lax
from jax.experimental import pallas as pl
from jax.experimental.pallas import tpu as pltpu
from jax.sharding import PartitionSpec as P

BLOCK_ROWS = 128
TPD = 2
F32 = jnp.float32
BF16 = jnp.bfloat16
VMEM_LIMIT = 24 * 1024 * 1024
TILE_VMEM = 16 * 1024 * 1024
SUM_VMEM = 8 * 1024 * 1024
PREPARE_CHUNK = 1024


def in_hbm(x):
    return pltpu.with_memory_space_constraint(x, pltpu.HBM)


def dot_nt(a, b):
    return lax.dot_general(a, b, (((1,), (1,)), ((), ())), preferred_element_type=F32)


def dot_nn(a, b):
    return lax.dot_general(a, b, (((1,), (0,)), ((), ())), preferred_element_type=F32)


def high_low(x):
    high = x.astype(BF16)
    return high, (x - high.astype(F32)).astype(BF16)


def prepare_kernel(half, where, own_pred, rem_pred, noise, observed, noise_var,
                   anom, base, keep, send1, send2, send3, diag_acc, left_acc, both_acc, scaled, stack):
    step = pl.program_id(0)
    group = where[0]
    chunk = own_pred.shape[1]
    strip = min(256, chunk)
    own_at = pl.multiple_of(group * half, half)
    rem_at = pl.multiple_of((1 - group) * half, half)
    quarter_at = pl.multiple_of(group * (half // 2), half // 2)
    deviation = jnp.sqrt(noise_var[...])
    inverse = 1.0 / deviation
    for c in range(0, chunk, strip):
        cols = slice(c, c + strip)
        own = own_pred[:, cols].astype(F32)
        rem = rem_pred[:, cols].astype(F32)
        mean = (jnp.sum(own, 0, keepdims=True) + jnp.sum(rem, 0, keepdims=True)) * (0.5 / half)
        own_anom = (own - mean).astype(BF16)
        rem_anom = (rem - mean).astype(BF16)
        scale = inverse[:, cols].astype(BF16)
        here = pl.ds(pl.multiple_of(step * chunk + c, strip), strip)
        anom[pl.ds(own_at, half), here] = own_anom
        anom[pl.ds(rem_at, half), here] = rem_anom
        scaled[pl.ds(own_at, half), cols] = own_anom * scale
        scaled[pl.ds(rem_at, half), cols] = rem_anom * scale
        forcing = (observed[:, cols] - mean) + deviation[:, cols] * noise[:, cols].astype(F32)
        forcing = forcing.astype(BF16)
        base[:, here] = forcing
        stack[0:half, cols] = forcing * scale
        stack[half:half * 3 // 2, cols] = scaled[pl.ds(quarter_at, half // 2), cols]
    own_scaled = scaled[pl.ds(own_at, half), :]
    diag = dot_nt(own_scaled, own_scaled)
    left = dot_nt(stack[0:half, :], scaled[0:half, :])
    both = dot_nt(stack[...], scaled[half:2 * half, :])

    @pl.when(step == 0)
    def _():
        diag_acc[...] = diag
        left_acc[...] = left
        both_acc[...] = both

    @pl.when(step != 0)
    def _():
        diag_acc[...] += diag
        left_acc[...] += left
        both_acc[...] += both

    @pl.when(step == pl.num_programs(0) - 1)
    def _():
        rows = half // 4
        for k, out in enumerate((keep, send1, send2, send3)):
            digit = jnp.bitwise_xor(where[1], k)
            rows_at = pl.ds(pl.multiple_of(digit * rows, rows), rows)
            off_at = pl.ds(pl.multiple_of(half + digit * (rows // 2), rows // 2), rows // 2)
            out[0:rows, :] = diag_acc[rows_at, :].astype(out.dtype)
            out[rows:rows * 3 // 2, :] = both_acc[off_at, :].astype(out.dtype)
            out[rows * 3 // 2:rows * 5 // 2, :] = left_acc[rows_at, :].astype(out.dtype)
            out[rows * 5 // 2:rows * 7 // 2, :] = both_acc[rows_at, :].astype(out.dtype)


def prepare(where, own_pred, rem_pred, noise, observed, noise_var):
    half, samples = own_pred.shape
    chunk = min(PREPARE_CHUNK, samples)
    column = lambda j: (0, j)
    fixed = lambda j: (0, 0)
    rows = half // 4 * 7 // 2
    return pl.pallas_call(
        functools.partial(prepare_kernel, half),
        grid=(samples // chunk,),
        in_specs=[
            pl.BlockSpec(memory_space=pltpu.SMEM),
            pl.BlockSpec((half, chunk), column),
            pl.BlockSpec((half, chunk), column),
            pl.BlockSpec((half, chunk), column),
            pl.BlockSpec((1, chunk), column),
            pl.BlockSpec((1, chunk), column),
        ],
        out_specs=[pl.BlockSpec(memory_space=pltpu.VMEM)] * 2 + [pl.BlockSpec((rows, half), fixed)] * 4,
        out_shape=[
            pltpu.VMEM((2 * half, samples), BF16),
            pltpu.VMEM((half, samples), BF16),
            jax.ShapeDtypeStruct((rows, half), F32),
        ]
        + [jax.ShapeDtypeStruct((rows, half), BF16)] * 3,
        scratch_shapes=[
            pltpu.VMEM((half, half), F32),
            pltpu.VMEM((half, half), F32),
            pltpu.VMEM((half * 3 // 2, half), F32),
            pltpu.VMEM((2 * half, chunk), BF16),
            pltpu.VMEM((half * 3 // 2, chunk), BF16),
        ],
        compiler_params=pltpu.CompilerParams(vmem_limit_bytes=VMEM_LIMIT),
        cost_estimate=pl.CostEstimate(
            flops=5 * half * half * samples, bytes_accessed=12 * half * samples, transcendentals=0
        ),
        name="prepare",
    )(where, in_hbm(own_pred), rem_pred, in_hbm(noise), in_hbm(observed.reshape(1, -1)),
      in_hbm(noise_var.reshape(1, -1)))


def sum_kernel(keep, *rest):
    *got, total, rounded = rest
    value = keep[...]
    for piece in got:
        value = value + piece[...].astype(F32)
    total[...] = value
    rounded[...] = value.astype(BF16)


def last_sum_kernel(keep, got, packed):
    value = keep[...] + got[...].astype(F32)
    rows = value.shape[0] * 2 // 7
    edge = rows * 3 // 2
    diag_hi, diag_lo = high_low(value[0:rows])
    off_hi, off_lo = high_low(value[rows:edge])
    packed[0:rows, :] = diag_hi
    packed[rows:2 * rows, :] = diag_lo
    packed[2 * rows:2 * rows + rows // 2, :] = off_hi
    packed[2 * rows + rows // 2:3 * rows, :] = off_lo
    packed[3 * rows:5 * rows, :] = value[edge:].astype(BF16)


def add_up(keep, got):
    return pl.pallas_call(
        sum_kernel,
        in_specs=[pl.BlockSpec(memory_space=pltpu.VMEM)] * (1 + len(got)),
        out_specs=[pl.BlockSpec(memory_space=pltpu.VMEM)] * 2,
        out_shape=[pltpu.VMEM(keep.shape, F32), pltpu.VMEM(keep.shape, BF16)],
        compiler_params=pltpu.CompilerParams(vmem_limit_bytes=SUM_VMEM),
        name="add_up",
    )(keep, *got)


def add_last(keep, got):
    half = keep.shape[1]
    return pl.pallas_call(
        last_sum_kernel,
        in_specs=[pl.BlockSpec(memory_space=pltpu.VMEM)] * 2,
        out_specs=pl.BlockSpec(memory_space=pltpu.VMEM),
        out_shape=pltpu.VMEM((half // 4 * 5, half), BF16),
        compiler_params=pltpu.CompilerParams(vmem_limit_bytes=SUM_VMEM),
        name="add_last",
    )(keep, got)


def exchange(value, distance):
    count = lax.axis_size("tile")
    return lax.ppermute(value, "tile", [(i, i ^ distance) for i in range(count)])


def swap_group(value):
    return lax.ppermute(value, "mem", [(0, 1), (1, 0)])


def tile_kernel(half, tiles, chunk, where, anom, base, scale, *rest):
    out, diag_acc, left_acc, both_acc, inner, outer = rest
    quarter = half // 2
    group = where[0]
    own_at = pl.multiple_of(group * half, half)
    quarter_at = pl.multiple_of(group * quarter, quarter)

    def terms(step):
        here = pl.ds(pl.multiple_of(step * chunk, chunk), chunk)
        own = anom[pl.ds(own_at, half), here]
        quarter_rows = anom[pl.ds(quarter_at, quarter), here]
        forcing = base[:, here]
        for t in range(tiles):
            weight = scale[t:t + 1, here].astype(BF16)
            inner[t * half:(t + 1) * half, :] = own * weight
            outer[t * half:(t + 1) * half, :] = forcing * weight
            at = tiles * half + t * quarter
            outer[at:at + quarter, :] = quarter_rows * weight
        diag = dot_nt(inner[...], own)
        left = dot_nt(outer[0:tiles * half, :], anom[0:half, here])
        both = dot_nt(outer[...], anom[half:2 * half, here])
        return diag, left, both

    diag_acc[...], left_acc[...], both_acc[...] = terms(0)

    @pl.loop(1, anom.shape[1] // chunk)
    def _(step):
        diag, left, both = terms(step)
        diag_acc[...] += diag
        left_acc[...] += left
        both_acc[...] += both

    for t in range(tiles):
        at = tiles * half + t * quarter
        own_rows = slice(t * half, (t + 1) * half)
        out[t, 0:half, :] = diag_acc[own_rows, :].astype(out.dtype)
        out[t, half:half + quarter, :] = both_acc[at:at + quarter, :].astype(out.dtype)
        out[t, half + quarter:2 * half + quarter, :] = left_acc[own_rows, :].astype(out.dtype)
        out[t, 2 * half + quarter:3 * half + quarter, :] = both_acc[own_rows, :].astype(out.dtype)


def tile_terms(where, anom, base, scale, kind):
    half, samples = base.shape
    tiles = scale.shape[0]
    chunk = min(1024, samples)
    rows = half * 7 // 2
    return pl.pallas_call(
        functools.partial(tile_kernel, half, tiles, chunk),
        in_specs=[pl.BlockSpec(memory_space=pltpu.SMEM)] + [pl.BlockSpec(memory_space=pltpu.VMEM)] * 3,
        out_specs=pl.BlockSpec(memory_space=pltpu.VMEM),
        out_shape=pltpu.VMEM((tiles, rows, half), kind),
        scratch_shapes=[
            pltpu.VMEM((tiles * half, half), F32),
            pltpu.VMEM((tiles * half, half), F32),
            pltpu.VMEM((tiles * half * 3 // 2, half), F32),
            pltpu.VMEM((tiles * half, chunk), BF16),
            pltpu.VMEM((tiles * half * 3 // 2, chunk), BF16),
        ],
        compiler_params=pltpu.CompilerParams(vmem_limit_bytes=TILE_VMEM),
        cost_estimate=pl.CostEstimate(
            flops=7 * half * half * samples * tiles, bytes_accessed=6 * half * samples, transcendentals=0
        ),
        name="tile_terms",
    )(where, anom, base, scale)


def solve_kernel(half, where, *refs):
    own_refs, rem_refs, out = refs[0:4], refs[4:8], refs[8]
    matrix, right, own_diag, rem_diag, own_off, rem_off = refs[9:]
    group = where[0]
    rows = half // 4
    members = 2 * half
    prior = members - 1.0
    for k in range(4):
        digit = jnp.bitwise_xor(where[1], k)
        diag_at = pl.ds(pl.multiple_of(digit * rows, rows), rows)
        off_at = pl.ds(pl.multiple_of(digit * (rows // 2), rows // 2), rows // 2)
        for refs_k, diag, off in ((own_refs, own_diag, own_off), (rem_refs, rem_diag, rem_off)):
            ens_part = refs_k[k][0:3 * rows, :].astype(F32)
            diag[diag_at, :] = ens_part[0:rows] + ens_part[rows:2 * rows]
            off[off_at, :] = ens_part[2 * rows:2 * rows + rows // 2] + ens_part[2 * rows + rows // 2:]
        right[diag_at, 0:half] = own_refs[k][3 * rows:4 * rows, :].astype(F32)
        right[diag_at, half:members] = own_refs[k][4 * rows:5 * rows, :].astype(F32)
    first = group == 0
    off = jnp.concatenate(
        [jnp.where(first, own_off[...], rem_off[...]), jnp.where(first, rem_off[...], own_off[...])], 0
    )
    row_at = lax.broadcasted_iota(jnp.int32, (half, half), 0)
    col_at = lax.broadcasted_iota(jnp.int32, (half, half), 1)
    eye = jnp.where(row_at == col_at, prior, 0.0)
    matrix[0:half, 0:half] = jnp.where(first, own_diag[...], rem_diag[...]) + eye
    matrix[half:members, half:members] = jnp.where(first, rem_diag[...], own_diag[...]) + eye
    matrix[0:half, half:members] = off
    matrix[half:members, 0:half] = off.T
    right[:, 0:half] += jnp.where(first, eye, 0.0)
    right[:, half:members] += jnp.where(first, 0.0, eye)

    whole = matrix[...]
    row_bound = jnp.max(jnp.sum(jnp.abs(whole), axis=1))
    top = jnp.minimum(row_bound, jnp.sqrt(jnp.sum(whole * whole))) * 1.0001
    factor = 2.0 / (top + prior)
    matrix[...] = whole * factor
    right[...] = right[...] * factor

    def update(spread):
        y = matrix[...]
        y_hi = y.astype(BF16)
        y_lo = (y - y_hi.astype(F32)).astype(BF16)
        c = right[...]
        c_hi = c.astype(BF16)
        c_lo = (c - c_hi.astype(F32)).astype(BF16)
        square = spread * spread
        s = 2.0 / (2.0 - square)
        matrix[...] = s * (2.0 * y - (dot_nn(y_hi, y_hi) + dot_nn(y_hi, y_lo) + dot_nn(y_lo, y_hi)))
        right[...] = s * (2.0 * c - (dot_nn(c_hi, y_hi) + dot_nn(c_hi, y_lo) + dot_nn(c_lo, y_hi)))
        return square / (2.0 - square)

    lax.while_loop(lambda spread: spread > 0.02, update, (top - prior) / (top + prior))
    y = matrix[...]
    y_hi = y.astype(BF16)
    y_lo = (y - y_hi.astype(F32)).astype(BF16)
    c = right[...]
    c_hi = c.astype(BF16)
    c_lo = (c - c_hi.astype(F32)).astype(BF16)
    last = 2.0 * c - (dot_nn(c_hi, y_hi) + dot_nn(c_hi, y_lo) + dot_nn(c_lo, y_hi))
    out[...] = last.astype(BF16)


def solve(where, own, rem):
    half = own[0].shape[1]
    return pl.pallas_call(
        functools.partial(solve_kernel, half),
        in_specs=[pl.BlockSpec(memory_space=pltpu.SMEM)] + [pl.BlockSpec(memory_space=pltpu.VMEM)] * 8,
        out_specs=pl.BlockSpec(memory_space=pltpu.VMEM),
        out_shape=jax.ShapeDtypeStruct((half, 2 * half), BF16),
        scratch_shapes=[
            pltpu.VMEM((2 * half, 2 * half), F32),
            pltpu.VMEM((half, 2 * half), F32),
            pltpu.VMEM((half, half), F32),
            pltpu.VMEM((half, half), F32),
            pltpu.VMEM((half // 2, half), F32),
            pltpu.VMEM((half // 2, half), F32),
        ],
        compiler_params=pltpu.CompilerParams(vmem_limit_bytes=VMEM_LIMIT),
        cost_estimate=pl.CostEstimate(
            flops=700 * half**3, bytes_accessed=16 * half * half, transcendentals=0
        ),
        name="solve",
    )(where, *own, *rem)


def finish_kernel(half, arrivals, where, coeffs, own_sum, rem_sum, own_prod, *rest):
    got = rest[:arrivals]
    own_model, rem_model, out, own_gain, rem_gain = rest[arrivals:]
    first = where[0] == 0

    @pl.when(pl.program_id(1) == 0)
    def _():
        own = own_sum[0]
        rem = rem_sum[0]
        top = jnp.where(first, own[0:half], rem[0:half])
        low = jnp.where(first, rem[0:half], own[0:half])
        off = jnp.concatenate(
            [
                jnp.where(first, own[half:], rem[half:]),
                jnp.where(first, rem[half:], own[half:]),
            ],
            0,
        )
        left_c = coeffs[:, 0:half]
        right_c = coeffs[:, half:2 * half]
        prod = own_prod[0, half * 3 // 2:, :]
        for piece in got:
            prod = prod + piece[0, half * 3 // 2:, :].astype(F32)
        scale = 1.0 / (2.0 * half - 1.0)
        left = (prod[0:half] - (dot_nn(left_c, top) + dot_nt(right_c, off))) * scale
        right = (prod[half:] - (dot_nn(left_c, off) + dot_nn(right_c, low))) * scale
        mean = (jnp.sum(left, 1, keepdims=True) + jnp.sum(right, 1, keepdims=True)) * (0.5 / half)
        left = (left - mean).astype(BF16)
        right = (right - mean).astype(BF16)
        own_gain[...] = jnp.where(first, left, right)
        rem_gain[...] = jnp.where(first, right, left)

    own = own_model[...]
    update = dot_nn(own_gain[...], own) + dot_nn(rem_gain[...], rem_model[...])
    out[...] = (own.astype(F32) + update).astype(BF16)


def finish(where, coeffs, own_sum, rem_sum, own_prod, got, own_model, rem_model):
    half, cells = own_model.shape
    chunk = min(1024, cells // TPD)
    steps = cells // TPD // chunk
    column = lambda t, j: (0, t * steps + j)
    tile = lambda t, j: (t, 0, 0)
    rows = half * 7 // 2
    return pl.pallas_call(
        functools.partial(finish_kernel, half, len(got)),
        grid=(TPD, steps),
        in_specs=[
            pl.BlockSpec(memory_space=pltpu.SMEM),
            pl.BlockSpec((half, 2 * half), lambda t, j: (0, 0)),
            pl.BlockSpec((1, half * 3 // 2, half), tile),
            pl.BlockSpec((1, half * 3 // 2, half), tile),
        ]
        + [pl.BlockSpec((1, rows, half), tile)] * (1 + len(got))
        + [pl.BlockSpec((half, chunk), column)] * 2,
        out_specs=pl.BlockSpec((half, chunk), column),
        out_shape=jax.ShapeDtypeStruct((half, cells), BF16),
        scratch_shapes=[pltpu.VMEM((half, half), BF16)] * 2,
        compiler_params=pltpu.CompilerParams(vmem_limit_bytes=VMEM_LIMIT),
        cost_estimate=pl.CostEstimate(
            flops=4 * half * half * cells, bytes_accessed=6 * half * cells, transcendentals=0
        ),
        name="finish",
    )(where, coeffs, own_sum, rem_sum, own_prod, *got, own_model, rem_model)


def sample_weights(block_lists, taper_weights, targets, source, inverse_var):
    blocks_local = inverse_var.shape[0] // BLOCK_ROWS
    rows = [lax.dynamic_slice_in_dim(block_lists, target * TPD, TPD, 0) for target in targets]
    tapers = [lax.dynamic_slice_in_dim(taper_weights, target * TPD, TPD, 0) for target in targets]
    rows, tapers = jnp.concatenate(rows, 0), jnp.concatenate(tapers, 0)
    ids = source * blocks_local + jnp.arange(blocks_local, dtype=jnp.int32)
    matches = rows[:, None, :] == ids[None, :, None]
    weights = jnp.sum(jnp.where(matches, tapers[:, None, :], 0.0), axis=2)
    scaled = weights[:, :, None] * inverse_var.reshape(1, blocks_local, BLOCK_ROWS)
    return scaled.reshape(rows.shape[0], -1)


def shards(ensemble, predicted, obs_noise, observed, noise_var, block_lists, taper_weights):
    half = predicted.shape[0]
    count = lax.axis_size("tile")
    index = lax.axis_index("tile")
    where = jnp.stack([lax.axis_index("mem"), index % 4]).astype(jnp.int32)
    rem_pred = swap_group(predicted)
    rem_model = swap_group(ensemble)

    reach = max(1, count // 16)
    if reach == 1:
        side = 1 - 2 * (index % 2)
        targets = [(index + side) % count, (index - side) % count]
        hops = [
            [(i, i ^ 1) for i in range(count)],
            [(i, (i + 2 * (i % 2) - 1) % count) for i in range(count)],
        ]
    else:
        offsets = [o for o in range(-reach, reach + 1) if o != 0]
        targets = [(index + o) % count for o in offsets]
        hops = [[(i, (i + o) % count) for i in range(count)] for o in offsets]
    scales = sample_weights(block_lists, taper_weights, targets + [index], index, 1.0 / noise_var)
    scales = [scales[n * TPD:(n + 1) * TPD] for n in range(len(targets) + 1)]

    anom, base, keep, *send = prepare(where, predicted, rem_pred, obs_noise, observed, noise_var)

    got = [exchange(send[k - 1], k) for k in (1, 2, 3)]
    near = tile_terms(where, anom, base, scales[0], BF16)
    got, near = lax.optimization_barrier((got, near))
    keep, packed = add_up(keep, got)
    arrivals = [lax.ppermute(near, "tile", hops[0])]
    bit = 4
    while bit < count:
        got = exchange(packed, bit)
        if 2 * bit >= count:
            later = [tile_terms(where, anom, base, scale, BF16) for scale in scales[1:-1]]
            got, later = lax.optimization_barrier((got, later))
        if 2 * bit >= count:
            packed = add_last(keep, got)
        else:
            keep, packed = add_up(keep, [got])
        bit *= 2
    own = [packed] + [exchange(packed, k) for k in (1, 2, 3)]
    own_terms = tile_terms(where, anom, base, scales[-1], F32)
    own[1], own_terms, later = lax.optimization_barrier((own[1], own_terms, later))
    own, arrivals = lax.optimization_barrier((own, arrivals))
    arrivals += [lax.ppermute(piece, "tile", hop) for piece, hop in zip(later, hops[1:])]
    rem = [swap_group(piece) for piece in own]
    coeffs = solve(where, own, rem)
    coeffs, arrivals = lax.optimization_barrier((coeffs, arrivals))

    own_sum = own_terms[:, :half * 3 // 2]
    for piece in arrivals:
        own_sum = own_sum + piece[:, :half * 3 // 2].astype(F32)
    own_sum = own_sum.astype(BF16)
    rem_sum = swap_group(own_sum)
    return finish(where, coeffs, own_sum, rem_sum, own_terms, arrivals, ensemble, rem_model)


def solution(mesh):
    in_specs = (
        P("mem", "tile"),
        P("mem", "tile"),
        P("mem", "tile"),
        P("tile"),
        P("tile"),
        P(),
        P(),
    )
    out_specs = P("mem", "tile")
    return jax.shard_map(shards, mesh=mesh, in_specs=in_specs, out_specs=out_specs, check_vma=False)
```

```python
import functools

import jax
import jax.numpy as jnp
from jax import lax
from jax.experimental import pallas as pl
from jax.experimental.pallas import tpu as pltpu
from jax.sharding import PartitionSpec as P

BLOCK_ROWS = 128
TPD = 2
F32 = jnp.float32
BF16 = jnp.bfloat16
VMEM_LIMIT = 24 * 1024 * 1024
TILE_VMEM = 16 * 1024 * 1024
SUM_VMEM = 8 * 1024 * 1024
PREPARE_CHUNK = 1024
ACROSS_EARLY = False


def in_hbm(x):
    return pltpu.with_memory_space_constraint(x, pltpu.HBM)


def dot_nt(a, b):
    return lax.dot_general(a, b, (((1,), (1,)), ((), ())), preferred_element_type=F32)


def dot_nn(a, b):
    return lax.dot_general(a, b, (((1,), (0,)), ((), ())), preferred_element_type=F32)


def high_low(x):
    high = x.astype(BF16)
    return high, (x - high.astype(F32)).astype(BF16)


def prepare_kernel(half, where, own_pred, rem_pred, noise, observed, noise_var,
                   anom, base, keep, send1, send2, send3, diag_acc, left_acc, both_acc, scaled, stack):
    step = pl.program_id(0)
    group = where[0]
    chunk = own_pred.shape[1]
    strip = min(256, chunk)
    own_at = pl.multiple_of(group * half, half)
    rem_at = pl.multiple_of((1 - group) * half, half)
    quarter_at = pl.multiple_of(group * (half // 2), half // 2)
    deviation = jnp.sqrt(noise_var[...])
    inverse = 1.0 / deviation
    for c in range(0, chunk, strip):
        cols = slice(c, c + strip)
        own = own_pred[:, cols].astype(F32)
        rem = rem_pred[:, cols].astype(F32)
        mean = (jnp.sum(own, 0, keepdims=True) + jnp.sum(rem, 0, keepdims=True)) * (0.5 / half)
        own_anom = (own - mean).astype(BF16)
        rem_anom = (rem - mean).astype(BF16)
        scale = inverse[:, cols].astype(BF16)
        here = pl.ds(pl.multiple_of(step * chunk + c, strip), strip)
        anom[pl.ds(own_at, half), here] = own_anom
        anom[pl.ds(rem_at, half), here] = rem_anom
        scaled[pl.ds(own_at, half), cols] = own_anom * scale
        scaled[pl.ds(rem_at, half), cols] = rem_anom * scale
        forcing = (observed[:, cols] - mean) + deviation[:, cols] * noise[:, cols].astype(F32)
        forcing = forcing.astype(BF16)
        base[:, here] = forcing
        stack[0:half, cols] = forcing * scale
        stack[half:half * 3 // 2, cols] = scaled[pl.ds(quarter_at, half // 2), cols]
    own_scaled = scaled[pl.ds(own_at, half), :]
    diag = dot_nt(own_scaled, own_scaled)
    left = dot_nt(stack[0:half, :], scaled[0:half, :])
    both = dot_nt(stack[...], scaled[half:2 * half, :])

    @pl.when(step == 0)
    def _():
        diag_acc[...] = diag
        left_acc[...] = left
        both_acc[...] = both

    @pl.when(step != 0)
    def _():
        diag_acc[...] += diag
        left_acc[...] += left
        both_acc[...] += both

    @pl.when(step == pl.num_programs(0) - 1)
    def _():
        rows = half // 4
        for k, out in enumerate((keep, send1, send2, send3)):
            digit = jnp.bitwise_xor(where[1], k)
            rows_at = pl.ds(pl.multiple_of(digit * rows, rows), rows)
            off_at = pl.ds(pl.multiple_of(half + digit * (rows // 2), rows // 2), rows // 2)
            out[0:rows, :] = diag_acc[rows_at, :].astype(out.dtype)
            out[rows:rows * 3 // 2, :] = both_acc[off_at, :].astype(out.dtype)
            out[rows * 3 // 2:rows * 5 // 2, :] = left_acc[rows_at, :].astype(out.dtype)
            out[rows * 5 // 2:rows * 7 // 2, :] = both_acc[rows_at, :].astype(out.dtype)


def prepare(where, own_pred, rem_pred, noise, observed, noise_var):
    half, samples = own_pred.shape
    chunk = min(PREPARE_CHUNK, samples)
    column = lambda j: (0, j)
    fixed = lambda j: (0, 0)
    rows = half // 4 * 7 // 2
    return pl.pallas_call(
        functools.partial(prepare_kernel, half),
        grid=(samples // chunk,),
        in_specs=[
            pl.BlockSpec(memory_space=pltpu.SMEM),
            pl.BlockSpec((half, chunk), column),
            pl.BlockSpec((half, chunk), column),
            pl.BlockSpec((half, chunk), column),
            pl.BlockSpec((1, chunk), column),
            pl.BlockSpec((1, chunk), column),
        ],
        out_specs=[pl.BlockSpec(memory_space=pltpu.VMEM)] * 2 + [pl.BlockSpec((rows, half), fixed)] * 4,
        out_shape=[
            pltpu.VMEM((2 * half, samples), BF16),
            pltpu.VMEM((half, samples), BF16),
            jax.ShapeDtypeStruct((rows, half), F32),
        ]
        + [jax.ShapeDtypeStruct((rows, half), BF16)] * 3,
        scratch_shapes=[
            pltpu.VMEM((half, half), F32),
            pltpu.VMEM((half, half), F32),
            pltpu.VMEM((half * 3 // 2, half), F32),
            pltpu.VMEM((2 * half, chunk), BF16),
            pltpu.VMEM((half * 3 // 2, chunk), BF16),
        ],
        compiler_params=pltpu.CompilerParams(vmem_limit_bytes=VMEM_LIMIT),
        cost_estimate=pl.CostEstimate(
            flops=5 * half * half * samples, bytes_accessed=12 * half * samples, transcendentals=0
        ),
        name="prepare",
    )(where, in_hbm(own_pred), rem_pred, in_hbm(noise), in_hbm(observed.reshape(1, -1)),
      in_hbm(noise_var.reshape(1, -1)))


def sum_kernel(keep, *rest):
    *got, total, rounded = rest
    value = keep[...]
    for piece in got:
        value = value + piece[...].astype(F32)
    total[...] = value
    rounded[...] = value.astype(BF16)


def last_sum_kernel(keep, got, packed):
    value = keep[...] + got[...].astype(F32)
    rows = value.shape[0] * 2 // 7
    edge = rows * 3 // 2
    diag_hi, diag_lo = high_low(value[0:rows])
    off_hi, off_lo = high_low(value[rows:edge])
    packed[0:rows, :] = diag_hi
    packed[rows:2 * rows, :] = diag_lo
    packed[2 * rows:2 * rows + rows // 2, :] = off_hi
    packed[2 * rows + rows // 2:3 * rows, :] = off_lo
    packed[3 * rows:5 * rows, :] = value[edge:].astype(BF16)


def add_up(keep, got):
    return pl.pallas_call(
        sum_kernel,
        in_specs=[pl.BlockSpec(memory_space=pltpu.VMEM)] * (1 + len(got)),
        out_specs=[pl.BlockSpec(memory_space=pltpu.VMEM)] * 2,
        out_shape=[pltpu.VMEM(keep.shape, F32), pltpu.VMEM(keep.shape, BF16)],
        compiler_params=pltpu.CompilerParams(vmem_limit_bytes=SUM_VMEM),
        name="add_up",
    )(keep, *got)


def add_last(keep, got):
    half = keep.shape[1]
    return pl.pallas_call(
        last_sum_kernel,
        in_specs=[pl.BlockSpec(memory_space=pltpu.VMEM)] * 2,
        out_specs=pl.BlockSpec(memory_space=pltpu.VMEM),
        out_shape=pltpu.VMEM((half // 4 * 5, half), BF16),
        compiler_params=pltpu.CompilerParams(vmem_limit_bytes=SUM_VMEM),
        name="add_last",
    )(keep, got)


def exchange(value, distance):
    count = lax.axis_size("tile")
    return lax.ppermute(value, "tile", [(i, i ^ distance) for i in range(count)])


def swap_group(value):
    return lax.ppermute(value, "mem", [(0, 1), (1, 0)])


def tile_kernel(half, tiles, chunk, where, anom, base, scale, *rest):
    outs = rest[:tiles]
    diag_acc, left_acc, both_acc, inner, outer = rest[tiles:]
    quarter = half // 2
    group = where[0]
    own_at = pl.multiple_of(group * half, half)
    quarter_at = pl.multiple_of(group * quarter, quarter)

    def terms(step):
        here = pl.ds(pl.multiple_of(step * chunk, chunk), chunk)
        own = anom[pl.ds(own_at, half), here]
        quarter_rows = anom[pl.ds(quarter_at, quarter), here]
        forcing = base[:, here]
        for t in range(tiles):
            weight = scale[t:t + 1, here].astype(BF16)
            inner[t * half:(t + 1) * half, :] = own * weight
            outer[t * half:(t + 1) * half, :] = forcing * weight
            at = tiles * half + t * quarter
            outer[at:at + quarter, :] = quarter_rows * weight
        diag = dot_nt(inner[...], own)
        left = dot_nt(outer[0:tiles * half, :], anom[0:half, here])
        both = dot_nt(outer[...], anom[half:2 * half, here])
        return diag, left, both

    diag_acc[...], left_acc[...], both_acc[...] = terms(0)

    @pl.loop(1, anom.shape[1] // chunk)
    def _(step):
        diag, left, both = terms(step)
        diag_acc[...] += diag
        left_acc[...] += left
        both_acc[...] += both

    for t, out in enumerate(outs):
        at = tiles * half + t * quarter
        own_rows = slice(t * half, (t + 1) * half)
        out[0:half, :] = diag_acc[own_rows, :].astype(out.dtype)
        out[half:half + quarter, :] = both_acc[at:at + quarter, :].astype(out.dtype)
        out[half + quarter:2 * half + quarter, :] = left_acc[own_rows, :].astype(out.dtype)
        out[2 * half + quarter:3 * half + quarter, :] = both_acc[own_rows, :].astype(out.dtype)


def tile_terms(where, anom, base, scale, kinds):
    half, samples = base.shape
    tiles = scale.shape[0]
    chunk = min(1024, samples)
    rows = half * 7 // 2
    return pl.pallas_call(
        functools.partial(tile_kernel, half, tiles, chunk),
        in_specs=[pl.BlockSpec(memory_space=pltpu.SMEM)] + [pl.BlockSpec(memory_space=pltpu.VMEM)] * 3,
        out_specs=[pl.BlockSpec(memory_space=pltpu.VMEM)] * tiles,
        out_shape=[pltpu.VMEM((rows, half), kind) for kind in kinds],
        scratch_shapes=[
            pltpu.VMEM((tiles * half, half), F32),
            pltpu.VMEM((tiles * half, half), F32),
            pltpu.VMEM((tiles * half * 3 // 2, half), F32),
            pltpu.VMEM((tiles * half, chunk), BF16),
            pltpu.VMEM((tiles * half * 3 // 2, chunk), BF16),
        ],
        compiler_params=pltpu.CompilerParams(vmem_limit_bytes=TILE_VMEM),
        cost_estimate=pl.CostEstimate(
            flops=7 * half * half * samples * tiles, bytes_accessed=6 * half * samples, transcendentals=0
        ),
        name="tile_terms",
    )(where, anom, base, scale)


def solve_kernel(half, where, *refs):
    own_refs, rem_refs, out = refs[0:4], refs[4:8], refs[8]
    matrix, right, own_diag, rem_diag, own_off, rem_off = refs[9:]
    group = where[0]
    rows = half // 4
    members = 2 * half
    prior = members - 1.0
    for k in range(4):
        digit = jnp.bitwise_xor(where[1], k)
        diag_at = pl.ds(pl.multiple_of(digit * rows, rows), rows)
        off_at = pl.ds(pl.multiple_of(digit * (rows // 2), rows // 2), rows // 2)
        for refs_k, diag, off in ((own_refs, own_diag, own_off), (rem_refs, rem_diag, rem_off)):
            ens_part = refs_k[k][0:3 * rows, :].astype(F32)
            diag[diag_at, :] = ens_part[0:rows] + ens_part[rows:2 * rows]
            off[off_at, :] = ens_part[2 * rows:2 * rows + rows // 2] + ens_part[2 * rows + rows // 2:]
        right[diag_at, 0:half] = own_refs[k][3 * rows:4 * rows, :].astype(F32)
        right[diag_at, half:members] = own_refs[k][4 * rows:5 * rows, :].astype(F32)
    first = group == 0
    off = jnp.concatenate(
        [jnp.where(first, own_off[...], rem_off[...]), jnp.where(first, rem_off[...], own_off[...])], 0
    )
    row_at = lax.broadcasted_iota(jnp.int32, (half, half), 0)
    col_at = lax.broadcasted_iota(jnp.int32, (half, half), 1)
    eye = jnp.where(row_at == col_at, prior, 0.0)
    matrix[0:half, 0:half] = jnp.where(first, own_diag[...], rem_diag[...]) + eye
    matrix[half:members, half:members] = jnp.where(first, rem_diag[...], own_diag[...]) + eye
    matrix[0:half, half:members] = off
    matrix[half:members, 0:half] = off.T
    right[:, 0:half] += jnp.where(first, eye, 0.0)
    right[:, half:members] += jnp.where(first, 0.0, eye)

    whole = matrix[...]
    row_bound = jnp.max(jnp.sum(jnp.abs(whole), axis=1))
    top = jnp.minimum(row_bound, jnp.sqrt(jnp.sum(whole * whole))) * 1.0001
    factor = 2.0 / (top + prior)
    matrix[...] = whole * factor
    right[...] = right[...] * factor

    def update(spread):
        y = matrix[...]
        y_hi = y.astype(BF16)
        y_lo = (y - y_hi.astype(F32)).astype(BF16)
        c = right[...]
        c_hi = c.astype(BF16)
        c_lo = (c - c_hi.astype(F32)).astype(BF16)
        square = spread * spread
        s = 2.0 / (2.0 - square)
        matrix[...] = s * (2.0 * y - (dot_nn(y_hi, y_hi) + dot_nn(y_hi, y_lo) + dot_nn(y_lo, y_hi)))
        right[...] = s * (2.0 * c - (dot_nn(c_hi, y_hi) + dot_nn(c_hi, y_lo) + dot_nn(c_lo, y_hi)))
        return square / (2.0 - square)

    lax.while_loop(lambda spread: spread > 0.02, update, (top - prior) / (top + prior))
    y = matrix[...]
    y_hi = y.astype(BF16)
    y_lo = (y - y_hi.astype(F32)).astype(BF16)
    c = right[...]
    c_hi = c.astype(BF16)
    c_lo = (c - c_hi.astype(F32)).astype(BF16)
    last = 2.0 * c - (dot_nn(c_hi, y_hi) + dot_nn(c_hi, y_lo) + dot_nn(c_lo, y_hi))
    out[...] = last.astype(BF16)


def solve(where, own, rem):
    half = own[0].shape[1]
    return pl.pallas_call(
        functools.partial(solve_kernel, half),
        in_specs=[pl.BlockSpec(memory_space=pltpu.SMEM)] + [pl.BlockSpec(memory_space=pltpu.VMEM)] * 8,
        out_specs=pl.BlockSpec(memory_space=pltpu.VMEM),
        out_shape=jax.ShapeDtypeStruct((half, 2 * half), BF16),
        scratch_shapes=[
            pltpu.VMEM((2 * half, 2 * half), F32),
            pltpu.VMEM((half, 2 * half), F32),
            pltpu.VMEM((half, half), F32),
            pltpu.VMEM((half, half), F32),
            pltpu.VMEM((half // 2, half), F32),
            pltpu.VMEM((half // 2, half), F32),
        ],
        compiler_params=pltpu.CompilerParams(vmem_limit_bytes=VMEM_LIMIT),
        cost_estimate=pl.CostEstimate(
            flops=700 * half**3, bytes_accessed=16 * half * half, transcendentals=0
        ),
        name="solve",
    )(where, *own, *rem)


def finish_kernel(half, arrivals, where, coeffs, own_sum, rem_sum, own_prod, *rest):
    got = rest[:arrivals]
    own_model, rem_model = rest[arrivals:arrivals + 2]
    out, own_gain, rem_gain = rest[-3:]
    first = where[0] == 0

    @pl.when(pl.program_id(0) == 0)
    def _():
        own = own_sum[...]
        rem = rem_sum[...]
        top = jnp.where(first, own[0:half], rem[0:half])
        low = jnp.where(first, rem[0:half], own[0:half])
        off = jnp.concatenate(
            [
                jnp.where(first, own[half:], rem[half:]),
                jnp.where(first, rem[half:], own[half:]),
            ],
            0,
        )
        left_c = coeffs[:, 0:half]
        right_c = coeffs[:, half:2 * half]
        prod = own_prod[half * 3 // 2:, :]
        for piece in got:
            prod = prod + piece[half * 3 // 2:, :].astype(F32)
        scale = 1.0 / (2.0 * half - 1.0)
        left = (prod[0:half] - (dot_nn(left_c, top) + dot_nt(right_c, off))) * scale
        right = (prod[half:] - (dot_nn(left_c, off) + dot_nn(right_c, low))) * scale
        mean = (jnp.sum(left, 1, keepdims=True) + jnp.sum(right, 1, keepdims=True)) * (0.5 / half)
        left = (left - mean).astype(BF16)
        right = (right - mean).astype(BF16)
        own_gain[...] = jnp.where(first, left, right)
        rem_gain[...] = jnp.where(first, right, left)

    own = own_model[...]
    update = dot_nn(own_gain[...], own) + dot_nn(rem_gain[...], rem_model[...])
    out[...] = (own.astype(F32) + update).astype(BF16)


def finish(tile, done, where, coeffs, own_sum, rem_sum, own_prod, got, own_model, rem_model):
    half, cells = own_model.shape
    chunk = min(1024, cells // TPD)
    steps = cells // TPD // chunk
    column = lambda j: (0, tile * steps + j)
    whole = lambda j: (0, 0)
    rows = half * 7 // 2
    operands = [where, coeffs, own_sum, rem_sum, own_prod, *got, own_model, rem_model]
    in_specs = (
        [
            pl.BlockSpec(memory_space=pltpu.SMEM),
            pl.BlockSpec((half, 2 * half), whole),
            pl.BlockSpec((half * 3 // 2, half), whole),
            pl.BlockSpec((half * 3 // 2, half), whole),
        ]
        + [pl.BlockSpec((rows, half), whole)] * (1 + len(got))
        + [pl.BlockSpec((half, chunk), column)] * 2
    )
    aliases = {}
    if done is not None:
        aliases = {len(operands): 0}
        operands.append(done)
        in_specs.append(pl.BlockSpec(memory_space=pl.ANY))
    return pl.pallas_call(
        functools.partial(finish_kernel, half, len(got)),
        grid=(steps,),
        in_specs=in_specs,
        out_specs=pl.BlockSpec((half, chunk), column),
        out_shape=jax.ShapeDtypeStruct((half, cells), BF16),
        input_output_aliases=aliases,
        scratch_shapes=[pltpu.VMEM((half, half), BF16)] * 2,
        compiler_params=pltpu.CompilerParams(vmem_limit_bytes=VMEM_LIMIT),
        cost_estimate=pl.CostEstimate(
            flops=4 * half * half * cells // TPD, bytes_accessed=6 * half * cells // TPD, transcendentals=0
        ),
        name="finish",
    )(*operands)


def sample_weights(block_lists, taper_weights, targets, source, inverse_var):
    blocks_local = inverse_var.shape[0] // BLOCK_ROWS
    rows = [lax.dynamic_slice_in_dim(block_lists, target * TPD, TPD, 0) for target in targets]
    tapers = [lax.dynamic_slice_in_dim(taper_weights, target * TPD, TPD, 0) for target in targets]
    rows, tapers = jnp.concatenate(rows, 0), jnp.concatenate(tapers, 0)
    ids = source * blocks_local + jnp.arange(blocks_local, dtype=jnp.int32)
    matches = rows[:, None, :] == ids[None, :, None]
    weights = jnp.sum(jnp.where(matches, tapers[:, None, :], 0.0), axis=2)
    scaled = weights[:, :, None] * inverse_var.reshape(1, blocks_local, BLOCK_ROWS)
    return scaled.reshape(rows.shape[0], -1)


def shards(ensemble, predicted, obs_noise, observed, noise_var, block_lists, taper_weights):
    half = predicted.shape[0]
    count = lax.axis_size("tile")
    index = lax.axis_index("tile")
    where = jnp.stack([lax.axis_index("mem"), index % 4]).astype(jnp.int32)
    rem_pred = swap_group(predicted)

    reach = max(1, count // 16)
    pair = [(i, i ^ 1) for i in range(count)]
    if reach == 1:
        side = 1 - 2 * (index % 2)
        offsets = [-side, side, 0]
    else:
        offsets = [o for o in range(-reach, reach + 1) if o != 0] + [0]
    targets = [(index + o) % count for o in offsets]
    scales = sample_weights(block_lists, taper_weights, targets, index, 1.0 / noise_var)
    scales = [scales[n * TPD:(n + 1) * TPD] for n in range(len(targets))]

    anom, base, keep, *send = prepare(where, predicted, rem_pred, obs_noise, observed, noise_var)
    terms = functools.partial(tile_terms, where, anom, base)
    send, model = lax.optimization_barrier((send, ensemble))
    rem_model = swap_group(model)

    got = [exchange(send[k - 1], k) for k in (1, 2, 3)]
    if reach == 1:
        far, near = scales[0], scales[1]
        far_first, near_second = terms(jnp.concatenate([far[0:1], near[1:2]], 0), (BF16, BF16))
        got, far_first, near_second = lax.optimization_barrier((got, far_first, near_second))
        hop = [(i, (i + 2) % count if i % 2 else (i - 2) % count) for i in range(count)]
        passed = lax.ppermute(far_first, "tile", hop)
        beside = lax.ppermute(near_second, "tile", pair)
    keep, packed = add_up(keep, got)
    bit = 4
    while 2 * bit < count:
        keep, packed = add_up(keep, [exchange(packed, bit)])
        bit *= 2
    if reach == 1:
        packed, mixed = lax.optimization_barrier((packed, jnp.concatenate([near[0:1], far[1:2]], 0)))
    got = exchange(packed, bit)
    if reach == 1:
        near_first, far_second = terms(mixed, (F32, BF16))
        got, near_first, far_second, passed = lax.optimization_barrier((got, near_first, far_second, passed))
        summed = (near_first + passed.astype(F32)).astype(BF16)
    packed = add_last(keep, got)
    packed, scales[-1] = lax.optimization_barrier((packed, scales[-1]))
    own = [packed] + [exchange(packed, k) for k in (1, 2, 3)]
    own_terms = terms(scales[-1], (F32,) * TPD)
    if reach == 1:
        if ACROSS_EARLY:
            across = lax.ppermute(summed, "tile", pair)
            own, own_terms, beside, far_second, across = lax.optimization_barrier(
                (own, own_terms, beside, far_second, across))
        else:
            own, own_terms, beside, far_second, summed = lax.optimization_barrier(
                (own, own_terms, beside, far_second, summed))
            across = lax.ppermute(summed, "tile", pair)
        away = [(i, (i + 2 * (i % 2) - 1) % count) for i in range(count)]
        arrivals = [[across], [beside, lax.ppermute(far_second, "tile", away)]]
    else:
        arrivals = [[] for _ in range(TPD)]
        for offset, scale in zip(offsets[:-1], scales):
            hop = [(i, (i + offset) % count) for i in range(count)]
            for pieces, piece in zip(arrivals, terms(scale, (BF16,) * TPD)):
                pieces.append(lax.ppermute(piece, "tile", hop))
    rem = [swap_group(piece) for piece in own]
    sums = []
    for t in range(TPD):
        if t == TPD - 1:
            coeffs = solve(where, own, rem)
            coeffs, arrivals[t] = lax.optimization_barrier((coeffs, arrivals[t]))
        own_sum = own_terms[t][:half * 3 // 2]
        for piece in arrivals[t]:
            own_sum = own_sum + piece[:half * 3 // 2].astype(F32)
        own_sum = own_sum.astype(BF16)
        sums.append((own_sum, swap_group(own_sum)))
    done = None
    for t in range(TPD):
        done = finish(t, done, where, coeffs, *sums[t], own_terms[t], arrivals[t], ensemble, rem_model)
    return done


def solution(mesh):
    in_specs = (
        P("mem", "tile"),
        P("mem", "tile"),
        P("mem", "tile"),
        P("tile"),
        P("tile"),
        P(),
        P(),
    )
    out_specs = P("mem", "tile")
    return jax.shard_map(shards, mesh=mesh, in_specs=in_specs, out_specs=out_specs, check_vma=False)
```

```python
import functools

import jax
import jax.numpy as jnp
from jax import lax
from jax.experimental import pallas as pl
from jax.experimental.pallas import tpu as pltpu
from jax.sharding import PartitionSpec as P

BLOCK_ROWS = 128
TPD = 2
F32 = jnp.float32
BF16 = jnp.bfloat16
VMEM_LIMIT = 24 * 1024 * 1024
TILE_VMEM = 16 * 1024 * 1024
SUM_VMEM = 8 * 1024 * 1024
PREPARE_CHUNK = 1024
ACROSS_EARLY = False


def in_hbm(x):
    return pltpu.with_memory_space_constraint(x, pltpu.HBM)


def dot_nt(a, b):
    return lax.dot_general(a, b, (((1,), (1,)), ((), ())), preferred_element_type=F32)


def dot_nn(a, b):
    return lax.dot_general(a, b, (((1,), (0,)), ((), ())), preferred_element_type=F32)


def high_low(x):
    high = x.astype(BF16)
    return high, (x - high.astype(F32)).astype(BF16)


def prepare_kernel(half, where, own_pred, rem_pred, noise, observed, noise_var,
                   anom, base, keep, send1, send2, send3, diag_acc, left_acc, both_acc, scaled, stack):
    step = pl.program_id(0)
    group = where[0]
    chunk = own_pred.shape[1]
    strip = min(256, chunk)
    own_at = pl.multiple_of(group * half, half)
    rem_at = pl.multiple_of((1 - group) * half, half)
    quarter_at = pl.multiple_of(group * (half // 2), half // 2)
    deviation = jnp.sqrt(noise_var[...])
    inverse = 1.0 / deviation
    for c in range(0, chunk, strip):
        cols = slice(c, c + strip)
        own = own_pred[:, cols].astype(F32)
        rem = rem_pred[:, cols].astype(F32)
        mean = (jnp.sum(own, 0, keepdims=True) + jnp.sum(rem, 0, keepdims=True)) * (0.5 / half)
        own_anom = (own - mean).astype(BF16)
        rem_anom = (rem - mean).astype(BF16)
        scale = inverse[:, cols].astype(BF16)
        here = pl.ds(pl.multiple_of(step * chunk + c, strip), strip)
        anom[pl.ds(own_at, half), here] = own_anom
        anom[pl.ds(rem_at, half), here] = rem_anom
        scaled[pl.ds(own_at, half), cols] = own_anom * scale
        scaled[pl.ds(rem_at, half), cols] = rem_anom * scale
        forcing = (observed[:, cols] - mean) + deviation[:, cols] * noise[:, cols].astype(F32)
        forcing = forcing.astype(BF16)
        base[:, here] = forcing
        stack[0:half, cols] = forcing * scale
        stack[half:half * 3 // 2, cols] = scaled[pl.ds(quarter_at, half // 2), cols]
    own_scaled = scaled[pl.ds(own_at, half), :]
    diag = dot_nt(own_scaled, own_scaled)
    left = dot_nt(stack[0:half, :], scaled[0:half, :])
    both = dot_nt(stack[...], scaled[half:2 * half, :])

    @pl.when(step == 0)
    def _():
        diag_acc[...] = diag
        left_acc[...] = left
        both_acc[...] = both

    @pl.when(step != 0)
    def _():
        diag_acc[...] += diag
        left_acc[...] += left
        both_acc[...] += both

    @pl.when(step == pl.num_programs(0) - 1)
    def _():
        rows = half // 4
        for k, out in enumerate((keep, send1, send2, send3)):
            digit = jnp.bitwise_xor(where[1], k)
            rows_at = pl.ds(pl.multiple_of(digit * rows, rows), rows)
            off_at = pl.ds(pl.multiple_of(half + digit * (rows // 2), rows // 2), rows // 2)
            out[0:rows, :] = diag_acc[rows_at, :].astype(out.dtype)
            out[rows:rows * 3 // 2, :] = both_acc[off_at, :].astype(out.dtype)
            out[rows * 3 // 2:rows * 5 // 2, :] = left_acc[rows_at, :].astype(out.dtype)
            out[rows * 5 // 2:rows * 7 // 2, :] = both_acc[rows_at, :].astype(out.dtype)


def prepare(where, own_pred, rem_pred, noise, observed, noise_var):
    half, samples = own_pred.shape
    chunk = min(PREPARE_CHUNK, samples)
    column = lambda j: (0, j)
    fixed = lambda j: (0, 0)
    rows = half // 4 * 7 // 2
    return pl.pallas_call(
        functools.partial(prepare_kernel, half),
        grid=(samples // chunk,),
        in_specs=[
            pl.BlockSpec(memory_space=pltpu.SMEM),
            pl.BlockSpec((half, chunk), column),
            pl.BlockSpec((half, chunk), column),
            pl.BlockSpec((half, chunk), column),
            pl.BlockSpec((1, chunk), column),
            pl.BlockSpec((1, chunk), column),
        ],
        out_specs=[pl.BlockSpec(memory_space=pltpu.VMEM)] * 2 + [pl.BlockSpec((rows, half), fixed)] * 4,
        out_shape=[
            pltpu.VMEM((2 * half, samples), BF16),
            pltpu.VMEM((half, samples), BF16),
            jax.ShapeDtypeStruct((rows, half), F32),
        ]
        + [jax.ShapeDtypeStruct((rows, half), BF16)] * 3,
        scratch_shapes=[
            pltpu.VMEM((half, half), F32),
            pltpu.VMEM((half, half), F32),
            pltpu.VMEM((half * 3 // 2, half), F32),
            pltpu.VMEM((2 * half, chunk), BF16),
            pltpu.VMEM((half * 3 // 2, chunk), BF16),
        ],
        compiler_params=pltpu.CompilerParams(vmem_limit_bytes=VMEM_LIMIT),
        cost_estimate=pl.CostEstimate(
            flops=5 * half * half * samples, bytes_accessed=12 * half * samples, transcendentals=0
        ),
        name="prepare",
    )(where, in_hbm(own_pred), rem_pred, in_hbm(noise), in_hbm(observed.reshape(1, -1)),
      in_hbm(noise_var.reshape(1, -1)))


def sum_kernel(keep, *rest):
    *got, total, rounded = rest
    value = keep[...]
    for piece in got:
        value = value + piece[...].astype(F32)
    total[...] = value
    rounded[...] = value.astype(BF16)


def last_sum_kernel(keep, got, packed):
    value = keep[...] + got[...].astype(F32)
    rows = value.shape[0] * 2 // 7
    edge = rows * 3 // 2
    diag_hi, diag_lo = high_low(value[0:rows])
    off_hi, off_lo = high_low(value[rows:edge])
    packed[0:rows, :] = diag_hi
    packed[rows:2 * rows, :] = diag_lo
    packed[2 * rows:2 * rows + rows // 2, :] = off_hi
    packed[2 * rows + rows // 2:3 * rows, :] = off_lo
    packed[3 * rows:5 * rows, :] = value[edge:].astype(BF16)


def add_up(keep, got):
    return pl.pallas_call(
        sum_kernel,
        in_specs=[pl.BlockSpec(memory_space=pltpu.VMEM)] * (1 + len(got)),
        out_specs=[pl.BlockSpec(memory_space=pltpu.VMEM)] * 2,
        out_shape=[pltpu.VMEM(keep.shape, F32), pltpu.VMEM(keep.shape, BF16)],
        compiler_params=pltpu.CompilerParams(vmem_limit_bytes=SUM_VMEM),
        name="add_up",
    )(keep, *got)


def add_last(keep, got):
    half = keep.shape[1]
    return pl.pallas_call(
        last_sum_kernel,
        in_specs=[pl.BlockSpec(memory_space=pltpu.VMEM)] * 2,
        out_specs=pl.BlockSpec(memory_space=pltpu.VMEM),
        out_shape=pltpu.VMEM((half // 4 * 5, half), BF16),
        compiler_params=pltpu.CompilerParams(vmem_limit_bytes=SUM_VMEM),
        name="add_last",
    )(keep, got)


def exchange(value, distance):
    count = lax.axis_size("tile")
    return lax.ppermute(value, "tile", [(i, i ^ distance) for i in range(count)])


def swap_group(value):
    return lax.ppermute(value, "mem", [(0, 1), (1, 0)])


def tile_kernel(half, tiles, chunk, where, anom, base, scale, *rest):
    outs = rest[:tiles]
    diag_acc, left_acc, both_acc, inner, outer = rest[tiles:]
    quarter = half // 2
    group = where[0]
    own_at = pl.multiple_of(group * half, half)
    quarter_at = pl.multiple_of(group * quarter, quarter)

    def terms(step):
        here = pl.ds(pl.multiple_of(step * chunk, chunk), chunk)
        own = anom[pl.ds(own_at, half), here]
        quarter_rows = anom[pl.ds(quarter_at, quarter), here]
        forcing = base[:, here]
        for t in range(tiles):
            weight = scale[t:t + 1, here].astype(BF16)
            inner[t * half:(t + 1) * half, :] = own * weight
            outer[t * half:(t + 1) * half, :] = forcing * weight
            at = tiles * half + t * quarter
            outer[at:at + quarter, :] = quarter_rows * weight
        diag = dot_nt(inner[...], own)
        left = dot_nt(outer[0:tiles * half, :], anom[0:half, here])
        both = dot_nt(outer[...], anom[half:2 * half, here])
        return diag, left, both

    diag_acc[...], left_acc[...], both_acc[...] = terms(0)

    @pl.loop(1, anom.shape[1] // chunk)
    def _(step):
        diag, left, both = terms(step)
        diag_acc[...] += diag
        left_acc[...] += left
        both_acc[...] += both

    piece = quarter // 2
    ens_rows = quarter + piece + quarter
    for t, out in enumerate(outs):
        at = tiles * half + t * quarter
        top = t * half
        middle = top + quarter
        own_rows = slice(top, top + half)
        out[0:quarter, 0:quarter] = diag_acc[top:middle, 0:quarter].astype(out.dtype)
        out[0:quarter, quarter:half] = diag_acc[middle:middle + quarter, quarter:half].astype(out.dtype)
        out[quarter:quarter + piece, 0:quarter] = diag_acc[top:top + piece, quarter:half].astype(out.dtype)
        out[quarter:quarter + piece, quarter:half] = diag_acc[top + piece:middle, quarter:half].astype(out.dtype)
        out[quarter + piece:ens_rows, :] = both_acc[at:at + quarter, :].astype(out.dtype)
        out[ens_rows:ens_rows + half, :] = left_acc[own_rows, :].astype(out.dtype)
        out[ens_rows + half:ens_rows + 2 * half, :] = both_acc[own_rows, :].astype(out.dtype)


def tile_terms(where, anom, base, scale, kinds):
    half, samples = base.shape
    tiles = scale.shape[0]
    chunk = min(1024, samples)
    rows = half * 13 // 4
    return pl.pallas_call(
        functools.partial(tile_kernel, half, tiles, chunk),
        in_specs=[pl.BlockSpec(memory_space=pltpu.SMEM)] + [pl.BlockSpec(memory_space=pltpu.VMEM)] * 3,
        out_specs=[pl.BlockSpec(memory_space=pltpu.VMEM)] * tiles,
        out_shape=[pltpu.VMEM((rows, half), kind) for kind in kinds],
        scratch_shapes=[
            pltpu.VMEM((tiles * half, half), F32),
            pltpu.VMEM((tiles * half, half), F32),
            pltpu.VMEM((tiles * half * 3 // 2, half), F32),
            pltpu.VMEM((tiles * half, chunk), BF16),
            pltpu.VMEM((tiles * half * 3 // 2, chunk), BF16),
        ],
        compiler_params=pltpu.CompilerParams(vmem_limit_bytes=TILE_VMEM),
        cost_estimate=pl.CostEstimate(
            flops=7 * half * half * samples * tiles, bytes_accessed=6 * half * samples, transcendentals=0
        ),
        name="tile_terms",
    )(where, anom, base, scale)


def solve_kernel(half, where, *refs):
    own_refs, rem_refs, out = refs[0:4], refs[4:8], refs[8]
    matrix, right, own_diag, rem_diag, own_off, rem_off = refs[9:]
    group = where[0]
    rows = half // 4
    members = 2 * half
    prior = members - 1.0
    for k in range(4):
        digit = jnp.bitwise_xor(where[1], k)
        diag_at = pl.ds(pl.multiple_of(digit * rows, rows), rows)
        off_at = pl.ds(pl.multiple_of(digit * (rows // 2), rows // 2), rows // 2)
        for refs_k, diag, off in ((own_refs, own_diag, own_off), (rem_refs, rem_diag, rem_off)):
            ens_part = refs_k[k][0:3 * rows, :].astype(F32)
            diag[diag_at, :] = ens_part[0:rows] + ens_part[rows:2 * rows]
            off[off_at, :] = ens_part[2 * rows:2 * rows + rows // 2] + ens_part[2 * rows + rows // 2:]
        right[diag_at, 0:half] = own_refs[k][3 * rows:4 * rows, :].astype(F32)
        right[diag_at, half:members] = own_refs[k][4 * rows:5 * rows, :].astype(F32)
    first = group == 0
    off = jnp.concatenate(
        [jnp.where(first, own_off[...], rem_off[...]), jnp.where(first, rem_off[...], own_off[...])], 0
    )
    row_at = lax.broadcasted_iota(jnp.int32, (half, half), 0)
    col_at = lax.broadcasted_iota(jnp.int32, (half, half), 1)
    eye = jnp.where(row_at == col_at, prior, 0.0)
    matrix[0:half, 0:half] = jnp.where(first, own_diag[...], rem_diag[...]) + eye
    matrix[half:members, half:members] = jnp.where(first, rem_diag[...], own_diag[...]) + eye
    matrix[0:half, half:members] = off
    matrix[half:members, 0:half] = off.T
    right[:, 0:half] += jnp.where(first, eye, 0.0)
    right[:, half:members] += jnp.where(first, 0.0, eye)

    whole = matrix[...]
    row_bound = jnp.max(jnp.sum(jnp.abs(whole), axis=1))
    top = jnp.minimum(row_bound, jnp.sqrt(jnp.sum(whole * whole))) * 1.0001
    factor = 2.0 / (top + prior)
    matrix[...] = whole * factor
    right[...] = right[...] * factor

    def update(spread):
        y = matrix[...]
        y_hi = y.astype(BF16)
        y_lo = (y - y_hi.astype(F32)).astype(BF16)
        c = right[...]
        c_hi = c.astype(BF16)
        c_lo = (c - c_hi.astype(F32)).astype(BF16)
        square = spread * spread
        s = 2.0 / (2.0 - square)
        matrix[...] = s * (2.0 * y - (dot_nn(y_hi, y_hi) + dot_nn(y_hi, y_lo) + dot_nn(y_lo, y_hi)))
        right[...] = s * (2.0 * c - (dot_nn(c_hi, y_hi) + dot_nn(c_hi, y_lo) + dot_nn(c_lo, y_hi)))
        return square / (2.0 - square)

    lax.while_loop(lambda spread: spread > 0.02, update, (top - prior) / (top + prior))
    y = matrix[...]
    y_hi = y.astype(BF16)
    y_lo = (y - y_hi.astype(F32)).astype(BF16)
    c = right[...]
    c_hi = c.astype(BF16)
    c_lo = (c - c_hi.astype(F32)).astype(BF16)
    last = 2.0 * c - (dot_nn(c_hi, y_hi) + dot_nn(c_hi, y_lo) + dot_nn(c_lo, y_hi))
    out[...] = last.astype(BF16)


def solve(where, own, rem):
    half = own[0].shape[1]
    return pl.pallas_call(
        functools.partial(solve_kernel, half),
        in_specs=[pl.BlockSpec(memory_space=pltpu.SMEM)] + [pl.BlockSpec(memory_space=pltpu.VMEM)] * 8,
        out_specs=pl.BlockSpec(memory_space=pltpu.VMEM),
        out_shape=jax.ShapeDtypeStruct((half, 2 * half), BF16),
        scratch_shapes=[
            pltpu.VMEM((2 * half, 2 * half), F32),
            pltpu.VMEM((half, 2 * half), F32),
            pltpu.VMEM((half, half), F32),
            pltpu.VMEM((half, half), F32),
            pltpu.VMEM((half // 2, half), F32),
            pltpu.VMEM((half // 2, half), F32),
        ],
        compiler_params=pltpu.CompilerParams(vmem_limit_bytes=VMEM_LIMIT),
        cost_estimate=pl.CostEstimate(
            flops=700 * half**3, bytes_accessed=16 * half * half, transcendentals=0
        ),
        name="solve",
    )(where, *own, *rem)


def finish_kernel(half, arrivals, where, coeffs, own_sum, rem_sum, own_prod, *rest):
    got = rest[:arrivals]
    own_model, rem_model = rest[arrivals:arrivals + 2]
    out, own_gain, rem_gain = rest[-3:]
    first = where[0] == 0

    @pl.when(pl.program_id(0) == 0)
    def _():
        quarter = half // 2
        piece = quarter // 2
        own = own_sum[...]
        rem = rem_sum[...]

        def diagonal(part):
            side = jnp.concatenate(
                [part[quarter:quarter + piece, 0:quarter], part[quarter:quarter + piece, quarter:half]], 0
            )
            upper = jnp.concatenate([part[0:quarter, 0:quarter], side], 1)
            lower = jnp.concatenate([side.T, part[0:quarter, quarter:half]], 1)
            return jnp.concatenate([upper, lower], 0)

        own_diag = diagonal(own)
        rem_diag = diagonal(rem)
        own_off = own[quarter + piece:]
        rem_off = rem[quarter + piece:]
        top = jnp.where(first, own_diag, rem_diag)
        low = jnp.where(first, rem_diag, own_diag)
        off = jnp.concatenate(
            [jnp.where(first, own_off, rem_off), jnp.where(first, rem_off, own_off)], 0
        )
        left_c = coeffs[:, 0:half]
        right_c = coeffs[:, half:2 * half]
        prod = own_prod[half * 5 // 4:, :]
        for more in got:
            prod = prod + more[half * 5 // 4:, :].astype(F32)
        scale = 1.0 / (2.0 * half - 1.0)
        left = (prod[0:half] - (dot_nn(left_c, top) + dot_nt(right_c, off))) * scale
        right = (prod[half:] - (dot_nn(left_c, off) + dot_nn(right_c, low))) * scale
        mean = (jnp.sum(left, 1, keepdims=True) + jnp.sum(right, 1, keepdims=True)) * (0.5 / half)
        left = (left - mean).astype(BF16)
        right = (right - mean).astype(BF16)
        own_gain[...] = jnp.where(first, left, right)
        rem_gain[...] = jnp.where(first, right, left)

    own = own_model[...]
    update = dot_nn(own_gain[...], own) + dot_nn(rem_gain[...], rem_model[...])
    out[...] = (own.astype(F32) + update).astype(BF16)


def finish(tile, done, where, coeffs, own_sum, rem_sum, own_prod, got, own_model, rem_model):
    half, cells = own_model.shape
    chunk = min(1024, cells // TPD)
    steps = cells // TPD // chunk
    column = lambda j: (0, tile * steps + j)
    whole = lambda j: (0, 0)
    rows = half * 13 // 4
    operands = [where, coeffs, own_sum, rem_sum, own_prod, *got, own_model, rem_model]
    in_specs = (
        [
            pl.BlockSpec(memory_space=pltpu.SMEM),
            pl.BlockSpec((half, 2 * half), whole),
            pl.BlockSpec((half * 5 // 4, half), whole),
            pl.BlockSpec((half * 5 // 4, half), whole),
        ]
        + [pl.BlockSpec((rows, half), whole)] * (1 + len(got))
        + [pl.BlockSpec((half, chunk), column)] * 2
    )
    aliases = {}
    if done is not None:
        aliases = {len(operands): 0}
        operands.append(done)
        in_specs.append(pl.BlockSpec(memory_space=pl.ANY))
    return pl.pallas_call(
        functools.partial(finish_kernel, half, len(got)),
        grid=(steps,),
        in_specs=in_specs,
        out_specs=pl.BlockSpec((half, chunk), column),
        out_shape=jax.ShapeDtypeStruct((half, cells), BF16),
        input_output_aliases=aliases,
        scratch_shapes=[pltpu.VMEM((half, half), BF16)] * 2,
        compiler_params=pltpu.CompilerParams(vmem_limit_bytes=VMEM_LIMIT),
        cost_estimate=pl.CostEstimate(
            flops=4 * half * half * cells // TPD, bytes_accessed=6 * half * cells // TPD, transcendentals=0
        ),
        name="finish",
    )(*operands)


def sample_weights(block_lists, taper_weights, targets, source, inverse_var):
    blocks_local = inverse_var.shape[0] // BLOCK_ROWS
    rows = [lax.dynamic_slice_in_dim(block_lists, target * TPD, TPD, 0) for target in targets]
    tapers = [lax.dynamic_slice_in_dim(taper_weights, target * TPD, TPD, 0) for target in targets]
    rows, tapers = jnp.concatenate(rows, 0), jnp.concatenate(tapers, 0)
    ids = source * blocks_local + jnp.arange(blocks_local, dtype=jnp.int32)
    matches = rows[:, None, :] == ids[None, :, None]
    weights = jnp.sum(jnp.where(matches, tapers[:, None, :], 0.0), axis=2)
    scaled = weights[:, :, None] * inverse_var.reshape(1, blocks_local, BLOCK_ROWS)
    return scaled.reshape(rows.shape[0], -1)


def shards(ensemble, predicted, obs_noise, observed, noise_var, block_lists, taper_weights):
    half = predicted.shape[0]
    count = lax.axis_size("tile")
    index = lax.axis_index("tile")
    where = jnp.stack([lax.axis_index("mem"), index % 4]).astype(jnp.int32)
    rem_pred = swap_group(predicted)

    reach = max(1, count // 16)
    pair = [(i, i ^ 1) for i in range(count)]
    if reach == 1:
        side = 1 - 2 * (index % 2)
        offsets = [-side, side, 0]
    else:
        offsets = [o for o in range(-reach, reach + 1) if o != 0] + [0]
    targets = [(index + o) % count for o in offsets]
    scales = sample_weights(block_lists, taper_weights, targets, index, 1.0 / noise_var)
    scales = [scales[n * TPD:(n + 1) * TPD] for n in range(len(targets))]

    anom, base, keep, *send = prepare(where, predicted, rem_pred, obs_noise, observed, noise_var)
    terms = functools.partial(tile_terms, where, anom, base)
    send, model = lax.optimization_barrier((send, ensemble))
    rem_model = swap_group(model)

    got = [exchange(send[k - 1], k) for k in (1, 2, 3)]
    if reach == 1:
        far, near = scales[0], scales[1]
        far_first, near_second = terms(jnp.concatenate([far[0:1], near[1:2]], 0), (BF16, BF16))
        got, far_first, near_second = lax.optimization_barrier((got, far_first, near_second))
        hop = [(i, (i + 2) % count if i % 2 else (i - 2) % count) for i in range(count)]
        passed = lax.ppermute(far_first, "tile", hop)
        beside = lax.ppermute(near_second, "tile", pair)
    keep, packed = add_up(keep, got)
    bit = 4
    while 2 * bit < count:
        keep, packed = add_up(keep, [exchange(packed, bit)])
        bit *= 2
    if reach == 1:
        packed, mixed = lax.optimization_barrier((packed, jnp.concatenate([near[0:1], far[1:2]], 0)))
    got = exchange(packed, bit)
    if reach == 1:
        near_first, far_second = terms(mixed, (F32, BF16))
        got, near_first, far_second, passed = lax.optimization_barrier((got, near_first, far_second, passed))
        summed = (near_first + passed.astype(F32)).astype(BF16)
    packed = add_last(keep, got)
    packed, scales[-1] = lax.optimization_barrier((packed, scales[-1]))
    own = [packed] + [exchange(packed, k) for k in (1, 2, 3)]
    own_terms = terms(scales[-1], (F32,) * TPD)
    if reach == 1:
        if ACROSS_EARLY:
            across = lax.ppermute(summed, "tile", pair)
            own, own_terms, beside, far_second, across = lax.optimization_barrier(
                (own, own_terms, beside, far_second, across))
        else:
            own, own_terms, beside, far_second, summed = lax.optimization_barrier(
                (own, own_terms, beside, far_second, summed))
            across = lax.ppermute(summed, "tile", pair)
        away = [(i, (i + 2 * (i % 2) - 1) % count) for i in range(count)]
        arrivals = [[across], [beside, lax.ppermute(far_second, "tile", away)]]
    else:
        arrivals = [[] for _ in range(TPD)]
        for offset, scale in zip(offsets[:-1], scales):
            hop = [(i, (i + offset) % count) for i in range(count)]
            for pieces, piece in zip(arrivals, terms(scale, (BF16,) * TPD)):
                pieces.append(lax.ppermute(piece, "tile", hop))
    rem = [swap_group(piece) for piece in own]
    sums = []
    for t in range(TPD):
        if t == TPD - 1:
            coeffs = solve(where, own, rem)
            coeffs, arrivals[t] = lax.optimization_barrier((coeffs, arrivals[t]))
        own_sum = own_terms[t][:half * 5 // 4]
        for piece in arrivals[t]:
            own_sum = own_sum + piece[:half * 5 // 4].astype(F32)
        own_sum = own_sum.astype(BF16)
        sums.append((own_sum, swap_group(own_sum)))
    done = None
    for t in range(TPD):
        done = finish(t, done, where, coeffs, *sums[t], own_terms[t], arrivals[t], ensemble, rem_model)
    return done


def solution(mesh):
    in_specs = (
        P("mem", "tile"),
        P("mem", "tile"),
        P("mem", "tile"),
        P("tile"),
        P("tile"),
        P(),
        P(),
    )
    out_specs = P("mem", "tile")
    return jax.shard_map(shards, mesh=mesh, in_specs=in_specs, out_specs=out_specs, check_vma=False)
```

```python
import functools

import jax
import jax.numpy as jnp
from jax import lax
from jax.experimental import pallas as pl
from jax.experimental.pallas import tpu as pltpu
from jax.sharding import PartitionSpec as P

BLOCK_ROWS = 128
TPD = 2
F32 = jnp.float32
BF16 = jnp.bfloat16
VMEM_LIMIT = 24 * 1024 * 1024
TILE_VMEM = 16 * 1024 * 1024
SUM_VMEM = 8 * 1024 * 1024
PREPARE_CHUNK = 1024
ACROSS_EARLY = False


def in_hbm(x):
    return pltpu.with_memory_space_constraint(x, pltpu.HBM)


def dot_nt(a, b):
    return lax.dot_general(a, b, (((1,), (1,)), ((), ())), preferred_element_type=F32)


def dot_nn(a, b):
    return lax.dot_general(a, b, (((1,), (0,)), ((), ())), preferred_element_type=F32)


def prepare_kernel(half, where, own_pred, rem_pred, noise, observed, noise_var,
                   anom, base, keep, send1, send2, send3, diag_acc, left_acc, both_acc, scaled, stack):
    step = pl.program_id(0)
    group = where[0]
    chunk = own_pred.shape[1]
    strip = min(256, chunk)
    own_at = pl.multiple_of(group * half, half)
    rem_at = pl.multiple_of((1 - group) * half, half)
    quarter_at = pl.multiple_of(group * (half // 2), half // 2)
    deviation = jnp.sqrt(noise_var[...])
    inverse = 1.0 / deviation
    for c in range(0, chunk, strip):
        cols = slice(c, c + strip)
        own = own_pred[:, cols].astype(F32)
        rem = rem_pred[:, cols].astype(F32)
        mean = (jnp.sum(own, 0, keepdims=True) + jnp.sum(rem, 0, keepdims=True)) * (0.5 / half)
        own_anom = (own - mean).astype(BF16)
        rem_anom = (rem - mean).astype(BF16)
        scale = inverse[:, cols].astype(BF16)
        here = pl.ds(pl.multiple_of(step * chunk + c, strip), strip)
        anom[pl.ds(own_at, half), here] = own_anom
        anom[pl.ds(rem_at, half), here] = rem_anom
        scaled[pl.ds(own_at, half), cols] = own_anom * scale
        scaled[pl.ds(rem_at, half), cols] = rem_anom * scale
        forcing = (observed[:, cols] - mean) + deviation[:, cols] * noise[:, cols].astype(F32)
        forcing = forcing.astype(BF16)
        base[:, here] = forcing
        stack[0:half, cols] = forcing * scale
        stack[half:half * 3 // 2, cols] = scaled[pl.ds(quarter_at, half // 2), cols]
    own_scaled = scaled[pl.ds(own_at, half), :]
    diag = dot_nt(own_scaled, own_scaled)
    left = dot_nt(stack[0:half, :], scaled[0:half, :])
    both = dot_nt(stack[...], scaled[half:2 * half, :])

    @pl.when(step == 0)
    def _():
        diag_acc[...] = diag
        left_acc[...] = left
        both_acc[...] = both

    @pl.when(step != 0)
    def _():
        diag_acc[...] += diag
        left_acc[...] += left
        both_acc[...] += both

    @pl.when(step == pl.num_programs(0) - 1)
    def _():
        rows = half // 4
        for k, out in enumerate((keep, send1, send2, send3)):
            digit = jnp.bitwise_xor(where[1], k)
            rows_at = pl.ds(pl.multiple_of(digit * rows, rows), rows)
            off_at = pl.ds(pl.multiple_of(half + digit * (rows // 2), rows // 2), rows // 2)
            out[0:rows, :] = diag_acc[rows_at, :].astype(out.dtype)
            out[rows:rows * 3 // 2, :] = both_acc[off_at, :].astype(out.dtype)
            out[rows * 3 // 2:rows * 5 // 2, :] = left_acc[rows_at, :].astype(out.dtype)
            out[rows * 5 // 2:rows * 7 // 2, :] = both_acc[rows_at, :].astype(out.dtype)


def prepare(where, own_pred, rem_pred, noise, observed, noise_var):
    half, samples = own_pred.shape
    chunk = min(PREPARE_CHUNK, samples)
    column = lambda j: (0, j)
    fixed = lambda j: (0, 0)
    rows = half // 4 * 7 // 2
    return pl.pallas_call(
        functools.partial(prepare_kernel, half),
        grid=(samples // chunk,),
        in_specs=[
            pl.BlockSpec(memory_space=pltpu.SMEM),
            pl.BlockSpec((half, chunk), column),
            pl.BlockSpec((half, chunk), column),
            pl.BlockSpec((half, chunk), column),
            pl.BlockSpec((1, chunk), column),
            pl.BlockSpec((1, chunk), column),
        ],
        out_specs=[pl.BlockSpec(memory_space=pltpu.VMEM)] * 2 + [pl.BlockSpec((rows, half), fixed)] * 4,
        out_shape=[
            pltpu.VMEM((2 * half, samples), BF16),
            pltpu.VMEM((half, samples), BF16),
            jax.ShapeDtypeStruct((rows, half), F32),
        ]
        + [jax.ShapeDtypeStruct((rows, half), BF16)] * 3,
        scratch_shapes=[
            pltpu.VMEM((half, half), F32),
            pltpu.VMEM((half, half), F32),
            pltpu.VMEM((half * 3 // 2, half), F32),
            pltpu.VMEM((2 * half, chunk), BF16),
            pltpu.VMEM((half * 3 // 2, chunk), BF16),
        ],
        compiler_params=pltpu.CompilerParams(vmem_limit_bytes=VMEM_LIMIT),
        cost_estimate=pl.CostEstimate(
            flops=5 * half * half * samples, bytes_accessed=12 * half * samples, transcendentals=0
        ),
        name="prepare",
    )(where, in_hbm(own_pred), rem_pred, in_hbm(noise), in_hbm(observed.reshape(1, -1)),
      in_hbm(noise_var.reshape(1, -1)))


def sum_kernel(keep, *rest):
    *got, total, rounded = rest
    value = keep[...]
    for piece in got:
        value = value + piece[...].astype(F32)
    total[...] = value
    rounded[...] = value.astype(BF16)


def add_up(keep, got):
    return pl.pallas_call(
        sum_kernel,
        in_specs=[pl.BlockSpec(memory_space=pltpu.VMEM)] * (1 + len(got)),
        out_specs=[pl.BlockSpec(memory_space=pltpu.VMEM)] * 2,
        out_shape=[pltpu.VMEM(keep.shape, F32), pltpu.VMEM(keep.shape, BF16)],
        compiler_params=pltpu.CompilerParams(vmem_limit_bytes=SUM_VMEM),
        name="add_up",
    )(keep, *got)


def exchange(value, distance):
    count = lax.axis_size("tile")
    return lax.ppermute(value, "tile", [(i, i ^ distance) for i in range(count)])


def swap_group(value):
    return lax.ppermute(value, "mem", [(0, 1), (1, 0)])


def tile_kernel(half, tiles, chunk, where, anom, base, scale, *rest):
    outs = rest[:tiles]
    diag_acc, left_acc, both_acc, inner, outer = rest[tiles:]
    quarter = half // 2
    group = where[0]
    own_at = pl.multiple_of(group * half, half)
    quarter_at = pl.multiple_of(group * quarter, quarter)

    def terms(step):
        here = pl.ds(pl.multiple_of(step * chunk, chunk), chunk)
        own = anom[pl.ds(own_at, half), here]
        quarter_rows = anom[pl.ds(quarter_at, quarter), here]
        forcing = base[:, here]
        for t in range(tiles):
            weight = scale[t:t + 1, here].astype(BF16)
            inner[t * half:(t + 1) * half, :] = own * weight
            outer[t * half:(t + 1) * half, :] = forcing * weight
            at = tiles * half + t * quarter
            outer[at:at + quarter, :] = quarter_rows * weight
        diag = dot_nt(inner[...], own)
        left = dot_nt(outer[0:tiles * half, :], anom[0:half, here])
        both = dot_nt(outer[...], anom[half:2 * half, here])
        return diag, left, both

    diag_acc[...], left_acc[...], both_acc[...] = terms(0)

    @pl.loop(1, anom.shape[1] // chunk)
    def _(step):
        diag, left, both = terms(step)
        diag_acc[...] += diag
        left_acc[...] += left
        both_acc[...] += both

    piece = quarter // 2
    ens_rows = quarter + piece + quarter
    for t, out in enumerate(outs):
        at = tiles * half + t * quarter
        top = t * half
        middle = top + quarter
        own_rows = slice(top, top + half)
        out[0:quarter, 0:quarter] = diag_acc[top:middle, 0:quarter].astype(out.dtype)
        out[0:quarter, quarter:half] = diag_acc[middle:middle + quarter, quarter:half].astype(out.dtype)
        out[quarter:quarter + piece, 0:quarter] = diag_acc[top:top + piece, quarter:half].astype(out.dtype)
        out[quarter:quarter + piece, quarter:half] = diag_acc[top + piece:middle, quarter:half].astype(out.dtype)
        out[quarter + piece:ens_rows, :] = both_acc[at:at + quarter, :].astype(out.dtype)
        out[ens_rows:ens_rows + half, :] = left_acc[own_rows, :].astype(out.dtype)
        out[ens_rows + half:ens_rows + 2 * half, :] = both_acc[own_rows, :].astype(out.dtype)


def tile_terms(where, anom, base, scale, kinds):
    half, samples = base.shape
    tiles = scale.shape[0]
    chunk = min(2048, samples)
    rows = half * 13 // 4
    return pl.pallas_call(
        functools.partial(tile_kernel, half, tiles, chunk),
        in_specs=[pl.BlockSpec(memory_space=pltpu.SMEM)] + [pl.BlockSpec(memory_space=pltpu.VMEM)] * 3,
        out_specs=[pl.BlockSpec(memory_space=pltpu.VMEM)] * tiles,
        out_shape=[pltpu.VMEM((rows, half), kind) for kind in kinds],
        scratch_shapes=[
            pltpu.VMEM((tiles * half, half), F32),
            pltpu.VMEM((tiles * half, half), F32),
            pltpu.VMEM((tiles * half * 3 // 2, half), F32),
            pltpu.VMEM((tiles * half, chunk), BF16),
            pltpu.VMEM((tiles * half * 3 // 2, chunk), BF16),
        ],
        compiler_params=pltpu.CompilerParams(vmem_limit_bytes=TILE_VMEM),
        cost_estimate=pl.CostEstimate(
            flops=7 * half * half * samples * tiles, bytes_accessed=6 * half * samples, transcendentals=0
        ),
        name="tile_terms",
    )(where, anom, base, scale)


def solve_kernel(half, where, *refs):
    own_refs, rem_refs, out = refs[0:4], refs[4:8], refs[8]
    matrix, right, own_diag, rem_diag, own_off, rem_off = refs[9:]
    group = where[0]
    rows = half // 4
    members = 2 * half
    prior = members - 1.0
    for k in range(4):
        digit = jnp.bitwise_xor(where[1], k)
        diag_at = pl.ds(pl.multiple_of(digit * rows, rows), rows)
        off_at = pl.ds(pl.multiple_of(digit * (rows // 2), rows // 2), rows // 2)
        edge = rows * 3 // 2
        for refs_k, diag, off in ((own_refs, own_diag, own_off), (rem_refs, rem_diag, rem_off)):
            diag[diag_at, :] = refs_k[k][0:rows, :].astype(F32)
            off[off_at, :] = refs_k[k][rows:edge, :].astype(F32)
        right[diag_at, 0:half] = own_refs[k][edge:edge + rows, :].astype(F32)
        right[diag_at, half:members] = own_refs[k][edge + rows:edge + 2 * rows, :].astype(F32)
    first = group == 0
    off = jnp.concatenate(
        [jnp.where(first, own_off[...], rem_off[...]), jnp.where(first, rem_off[...], own_off[...])], 0
    )
    row_at = lax.broadcasted_iota(jnp.int32, (half, half), 0)
    col_at = lax.broadcasted_iota(jnp.int32, (half, half), 1)
    eye = jnp.where(row_at == col_at, prior, 0.0)
    matrix[0:half, 0:half] = jnp.where(first, own_diag[...], rem_diag[...]) + eye
    matrix[half:members, half:members] = jnp.where(first, rem_diag[...], own_diag[...]) + eye
    matrix[0:half, half:members] = off
    matrix[half:members, 0:half] = off.T
    right[:, 0:half] += jnp.where(first, eye, 0.0)
    right[:, half:members] += jnp.where(first, 0.0, eye)

    whole = matrix[...]
    row_bound = jnp.max(jnp.sum(jnp.abs(whole), axis=1))
    top = jnp.minimum(row_bound, jnp.sqrt(jnp.sum(whole * whole))) * 1.0001
    factor = 2.0 / (top + prior)
    matrix[...] = whole * factor
    right[...] = right[...] * factor

    def update(spread):
        y = matrix[...]
        y_hi = y.astype(BF16)
        y_lo = (y - y_hi.astype(F32)).astype(BF16)
        c = right[...]
        c_hi = c.astype(BF16)
        c_lo = (c - c_hi.astype(F32)).astype(BF16)
        square = spread * spread
        s = 2.0 / (2.0 - square)
        matrix[...] = s * (2.0 * y - (dot_nn(y_hi, y_hi) + dot_nn(y_hi, y_lo) + dot_nn(y_lo, y_hi)))
        right[...] = s * (2.0 * c - (dot_nn(c_hi, y_hi) + dot_nn(c_hi, y_lo) + dot_nn(c_lo, y_hi)))
        return square / (2.0 - square)

    lax.while_loop(lambda spread: spread > 0.02, update, (top - prior) / (top + prior))
    y = matrix[...]
    y_hi = y.astype(BF16)
    y_lo = (y - y_hi.astype(F32)).astype(BF16)
    c = right[...]
    c_hi = c.astype(BF16)
    c_lo = (c - c_hi.astype(F32)).astype(BF16)
    last = 2.0 * c - (dot_nn(c_hi, y_hi) + dot_nn(c_hi, y_lo) + dot_nn(c_lo, y_hi))
    out[...] = last.astype(BF16)


def solve(where, own, rem):
    half = own[0].shape[1]
    return pl.pallas_call(
        functools.partial(solve_kernel, half),
        in_specs=[pl.BlockSpec(memory_space=pltpu.SMEM)] + [pl.BlockSpec(memory_space=pltpu.VMEM)] * 8,
        out_specs=pl.BlockSpec(memory_space=pltpu.VMEM),
        out_shape=jax.ShapeDtypeStruct((half, 2 * half), BF16),
        scratch_shapes=[
            pltpu.VMEM((2 * half, 2 * half), F32),
            pltpu.VMEM((half, 2 * half), F32),
            pltpu.VMEM((half, half), F32),
            pltpu.VMEM((half, half), F32),
            pltpu.VMEM((half // 2, half), F32),
            pltpu.VMEM((half // 2, half), F32),
        ],
        compiler_params=pltpu.CompilerParams(vmem_limit_bytes=VMEM_LIMIT),
        cost_estimate=pl.CostEstimate(
            flops=700 * half**3, bytes_accessed=16 * half * half, transcendentals=0
        ),
        name="solve",
    )(where, *own, *rem)


def finish_kernel(half, arrivals, where, coeffs, own_sum, rem_sum, own_prod, *rest):
    got = rest[:arrivals]
    own_model, rem_model = rest[arrivals:arrivals + 2]
    out, own_gain, rem_gain = rest[-3:]
    first = where[0] == 0

    @pl.when(pl.program_id(0) == 0)
    def _():
        quarter = half // 2
        piece = quarter // 2
        own = own_sum[...]
        rem = rem_sum[...]

        def diagonal(part):
            side = jnp.concatenate(
                [part[quarter:quarter + piece, 0:quarter], part[quarter:quarter + piece, quarter:half]], 0
            )
            upper = jnp.concatenate([part[0:quarter, 0:quarter], side], 1)
            lower = jnp.concatenate([side.T, part[0:quarter, quarter:half]], 1)
            return jnp.concatenate([upper, lower], 0)

        own_diag = diagonal(own)
        rem_diag = diagonal(rem)
        own_off = own[quarter + piece:]
        rem_off = rem[quarter + piece:]
        top = jnp.where(first, own_diag, rem_diag)
        low = jnp.where(first, rem_diag, own_diag)
        off = jnp.concatenate(
            [jnp.where(first, own_off, rem_off), jnp.where(first, rem_off, own_off)], 0
        )
        left_c = coeffs[:, 0:half]
        right_c = coeffs[:, half:2 * half]
        prod = own_prod[half * 5 // 4:, :]
        for more in got:
            prod = prod + more[half * 5 // 4:, :].astype(F32)
        scale = 1.0 / (2.0 * half - 1.0)
        left = (prod[0:half] - (dot_nn(left_c, top) + dot_nt(right_c, off))) * scale
        right = (prod[half:] - (dot_nn(left_c, off) + dot_nn(right_c, low))) * scale
        mean = (jnp.sum(left, 1, keepdims=True) + jnp.sum(right, 1, keepdims=True)) * (0.5 / half)
        left = (left - mean).astype(BF16)
        right = (right - mean).astype(BF16)
        own_gain[...] = jnp.where(first, left, right)
        rem_gain[...] = jnp.where(first, right, left)

    own = own_model[...]
    update = dot_nn(own_gain[...], own) + dot_nn(rem_gain[...], rem_model[...])
    out[...] = (own.astype(F32) + update).astype(BF16)


def finish(tile, done, where, coeffs, own_sum, rem_sum, own_prod, got, own_model, rem_model):
    half, cells = own_model.shape
    chunk = min(1024, cells // TPD)
    steps = cells // TPD // chunk
    column = lambda j: (0, tile * steps + j)
    whole = lambda j: (0, 0)
    rows = half * 13 // 4
    operands = [where, coeffs, own_sum, rem_sum, own_prod, *got, own_model, rem_model]
    in_specs = (
        [
            pl.BlockSpec(memory_space=pltpu.SMEM),
            pl.BlockSpec((half, 2 * half), whole),
            pl.BlockSpec((half * 5 // 4, half), whole),
            pl.BlockSpec((half * 5 // 4, half), whole),
        ]
        + [pl.BlockSpec((rows, half), whole)] * (1 + len(got))
        + [pl.BlockSpec((half, chunk), column)] * 2
    )
    aliases = {}
    if done is not None:
        aliases = {len(operands): 0}
        operands.append(done)
        in_specs.append(pl.BlockSpec(memory_space=pl.ANY))
    return pl.pallas_call(
        functools.partial(finish_kernel, half, len(got)),
        grid=(steps,),
        in_specs=in_specs,
        out_specs=pl.BlockSpec((half, chunk), column),
        out_shape=jax.ShapeDtypeStruct((half, cells), BF16),
        input_output_aliases=aliases,
        scratch_shapes=[pltpu.VMEM((half, half), BF16)] * 2,
        compiler_params=pltpu.CompilerParams(vmem_limit_bytes=VMEM_LIMIT),
        cost_estimate=pl.CostEstimate(
            flops=4 * half * half * cells // TPD, bytes_accessed=6 * half * cells // TPD, transcendentals=0
        ),
        name="finish",
    )(*operands)


def sample_weights(block_lists, taper_weights, targets, source, inverse_var):
    blocks_local = inverse_var.shape[0] // BLOCK_ROWS
    rows = [lax.dynamic_slice_in_dim(block_lists, target * TPD, TPD, 0) for target in targets]
    tapers = [lax.dynamic_slice_in_dim(taper_weights, target * TPD, TPD, 0) for target in targets]
    rows, tapers = jnp.concatenate(rows, 0), jnp.concatenate(tapers, 0)
    ids = source * blocks_local + jnp.arange(blocks_local, dtype=jnp.int32)
    matches = rows[:, None, :] == ids[None, :, None]
    weights = jnp.sum(jnp.where(matches, tapers[:, None, :], 0.0), axis=2)
    scaled = weights[:, :, None] * inverse_var.reshape(1, blocks_local, BLOCK_ROWS)
    return scaled.reshape(rows.shape[0], -1)


def shards(ensemble, predicted, obs_noise, observed, noise_var, block_lists, taper_weights):
    half = predicted.shape[0]
    count = lax.axis_size("tile")
    index = lax.axis_index("tile")
    where = jnp.stack([lax.axis_index("mem"), index % 4]).astype(jnp.int32)
    rem_pred = swap_group(predicted)

    reach = max(1, count // 16)
    pair = [(i, i ^ 1) for i in range(count)]
    if reach == 1:
        side = 1 - 2 * (index % 2)
        offsets = [-side, side, 0]
    else:
        offsets = [o for o in range(-reach, reach + 1) if o != 0] + [0]
    targets = [(index + o) % count for o in offsets]
    scales = sample_weights(block_lists, taper_weights, targets, index, 1.0 / noise_var)
    scales = [scales[n * TPD:(n + 1) * TPD] for n in range(len(targets))]

    anom, base, keep, *send = prepare(where, predicted, rem_pred, obs_noise, observed, noise_var)
    terms = functools.partial(tile_terms, where, anom, base)
    send, model = lax.optimization_barrier((send, ensemble))
    rem_model = swap_group(model)

    got = [exchange(send[k - 1], k) for k in (1, 2, 3)]
    if reach == 1:
        far, near = scales[0], scales[1]
        far_first, near_second = terms(jnp.concatenate([far[0:1], near[1:2]], 0), (BF16, BF16))
        got, far_first, near_second = lax.optimization_barrier((got, far_first, near_second))
        hop = [(i, (i + 2) % count if i % 2 else (i - 2) % count) for i in range(count)]
        passed = lax.ppermute(far_first, "tile", hop)
        beside = lax.ppermute(near_second, "tile", pair)
    keep, packed = add_up(keep, got)
    bit = 4
    while 2 * bit < count:
        keep, packed = add_up(keep, [exchange(packed, bit)])
        bit *= 2
    if reach == 1:
        packed, mixed = lax.optimization_barrier((packed, jnp.concatenate([near[0:1], far[1:2]], 0)))
    got = exchange(packed, bit)
    if reach == 1:
        near_first, far_second = terms(mixed, (F32, BF16))
        got, near_first, far_second, passed = lax.optimization_barrier((got, near_first, far_second, passed))
        summed = (near_first + passed.astype(F32)).astype(BF16)
    _, packed = add_up(keep, [got])
    packed, scales[-1] = lax.optimization_barrier((packed, scales[-1]))
    own = [packed] + [exchange(packed, k) for k in (1, 2, 3)]
    own_terms = terms(scales[-1], (F32,) * TPD)
    if reach == 1:
        if ACROSS_EARLY:
            across = lax.ppermute(summed, "tile", pair)
            own, own_terms, beside, far_second, across = lax.optimization_barrier(
                (own, own_terms, beside, far_second, across))
        else:
            own, own_terms, beside, far_second, summed = lax.optimization_barrier(
                (own, own_terms, beside, far_second, summed))
            across = lax.ppermute(summed, "tile", pair)
        away = [(i, (i + 2 * (i % 2) - 1) % count) for i in range(count)]
        arrivals = [[across], [beside, lax.ppermute(far_second, "tile", away)]]
    else:
        arrivals = [[] for _ in range(TPD)]
        for offset, scale in zip(offsets[:-1], scales):
            hop = [(i, (i + offset) % count) for i in range(count)]
            for pieces, piece in zip(arrivals, terms(scale, (BF16,) * TPD)):
                pieces.append(lax.ppermute(piece, "tile", hop))
    rem = [swap_group(piece) for piece in own]
    sums = []
    for t in range(TPD):
        if t == TPD - 1:
            coeffs = solve(where, own, rem)
            coeffs, arrivals[t] = lax.optimization_barrier((coeffs, arrivals[t]))
        own_sum = own_terms[t][:half * 5 // 4]
        for piece in arrivals[t]:
            own_sum = own_sum + piece[:half * 5 // 4].astype(F32)
        own_sum = own_sum.astype(BF16)
        sums.append((own_sum, swap_group(own_sum)))
    done = None
    for t in range(TPD):
        done = finish(t, done, where, coeffs, *sums[t], own_terms[t], arrivals[t], ensemble, rem_model)
    return done


def solution(mesh):
    in_specs = (
        P("mem", "tile"),
        P("mem", "tile"),
        P("mem", "tile"),
        P("tile"),
        P("tile"),
        P(),
        P(),
    )
    out_specs = P("mem", "tile")
    return jax.shard_map(shards, mesh=mesh, in_specs=in_specs, out_specs=out_specs, check_vma=False)
```

```python
import functools

import jax
import jax.numpy as jnp
from jax import lax
from jax.experimental import pallas as pl
from jax.experimental.pallas import tpu as pltpu
from jax.sharding import PartitionSpec as P

BLOCK_ROWS = 128
TPD = 2
F32 = jnp.float32
BF16 = jnp.bfloat16
VMEM_LIMIT = 24 * 1024 * 1024
TILE_VMEM = 16 * 1024 * 1024
SUM_VMEM = 8 * 1024 * 1024
PREPARE_CHUNK = 2048
ACROSS_EARLY = False


def in_hbm(x):
    return pltpu.with_memory_space_constraint(x, pltpu.HBM)


def dot_nt(a, b):
    return lax.dot_general(a, b, (((1,), (1,)), ((), ())), preferred_element_type=F32)


def dot_nn(a, b):
    return lax.dot_general(a, b, (((1,), (0,)), ((), ())), preferred_element_type=F32)


def prepare_kernel(half, where, own_pred, rem_pred, noise, observed, noise_var,
                   anom, base, keep, send1, send2, send3, diag_acc, left_acc, both_acc, scaled, stack):
    step = pl.program_id(0)
    group = where[0]
    chunk = own_pred.shape[1]
    strip = min(256, chunk)
    own_at = pl.multiple_of(group * half, half)
    rem_at = pl.multiple_of((1 - group) * half, half)
    quarter_at = pl.multiple_of(group * (half // 2), half // 2)
    deviation = jnp.sqrt(noise_var[...])
    inverse = 1.0 / deviation
    for c in range(0, chunk, strip):
        cols = slice(c, c + strip)
        own = own_pred[:, cols].astype(F32)
        rem = rem_pred[:, cols].astype(F32)
        mean = (jnp.sum(own, 0, keepdims=True) + jnp.sum(rem, 0, keepdims=True)) * (0.5 / half)
        own_anom = (own - mean).astype(BF16)
        rem_anom = (rem - mean).astype(BF16)
        scale = inverse[:, cols].astype(BF16)
        here = pl.ds(pl.multiple_of(step * chunk + c, strip), strip)
        anom[pl.ds(own_at, half), here] = own_anom
        anom[pl.ds(rem_at, half), here] = rem_anom
        scaled[pl.ds(own_at, half), cols] = own_anom * scale
        scaled[pl.ds(rem_at, half), cols] = rem_anom * scale
        forcing = (observed[:, cols] - mean) + deviation[:, cols] * noise[:, cols].astype(F32)
        forcing = forcing.astype(BF16)
        base[:, here] = forcing
        stack[0:half, cols] = forcing * scale
        stack[half:half * 3 // 2, cols] = scaled[pl.ds(quarter_at, half // 2), cols]
    own_scaled = scaled[pl.ds(own_at, half), :]
    diag = dot_nt(own_scaled, own_scaled)
    left = dot_nt(stack[0:half, :], scaled[0:half, :])
    both = dot_nt(stack[...], scaled[half:2 * half, :])

    @pl.when(step == 0)
    def _():
        diag_acc[...] = diag
        left_acc[...] = left
        both_acc[...] = both

    @pl.when(step != 0)
    def _():
        diag_acc[...] += diag
        left_acc[...] += left
        both_acc[...] += both

    @pl.when(step == pl.num_programs(0) - 1)
    def _():
        rows = half // 4
        for k, out in enumerate((keep, send1, send2, send3)):
            digit = jnp.bitwise_xor(where[1], k)
            rows_at = pl.ds(pl.multiple_of(digit * rows, rows), rows)
            off_at = pl.ds(pl.multiple_of(half + digit * (rows // 2), rows // 2), rows // 2)
            out[0:rows, :] = diag_acc[rows_at, :].astype(out.dtype)
            out[rows:rows * 3 // 2, :] = both_acc[off_at, :].astype(out.dtype)
            out[rows * 3 // 2:rows * 5 // 2, :] = left_acc[rows_at, :].astype(out.dtype)
            out[rows * 5 // 2:rows * 7 // 2, :] = both_acc[rows_at, :].astype(out.dtype)


def prepare(where, own_pred, rem_pred, noise, observed, noise_var):
    half, samples = own_pred.shape
    chunk = min(PREPARE_CHUNK, samples)
    column = lambda j: (0, j)
    fixed = lambda j: (0, 0)
    rows = half // 4 * 7 // 2
    return pl.pallas_call(
        functools.partial(prepare_kernel, half),
        grid=(samples // chunk,),
        in_specs=[
            pl.BlockSpec(memory_space=pltpu.SMEM),
            pl.BlockSpec((half, chunk), column),
            pl.BlockSpec((half, chunk), column),
            pl.BlockSpec((half, chunk), column),
            pl.BlockSpec((1, chunk), column),
            pl.BlockSpec((1, chunk), column),
        ],
        out_specs=[pl.BlockSpec(memory_space=pltpu.VMEM)] * 2 + [pl.BlockSpec((rows, half), fixed)] * 4,
        out_shape=[
            pltpu.VMEM((2 * half, samples), BF16),
            pltpu.VMEM((half, samples), BF16),
            jax.ShapeDtypeStruct((rows, half), F32),
        ]
        + [jax.ShapeDtypeStruct((rows, half), BF16)] * 3,
        scratch_shapes=[
            pltpu.VMEM((half, half), F32),
            pltpu.VMEM((half, half), F32),
            pltpu.VMEM((half * 3 // 2, half), F32),
            pltpu.VMEM((2 * half, chunk), BF16),
            pltpu.VMEM((half * 3 // 2, chunk), BF16),
        ],
        compiler_params=pltpu.CompilerParams(vmem_limit_bytes=VMEM_LIMIT),
        cost_estimate=pl.CostEstimate(
            flops=5 * half * half * samples, bytes_accessed=12 * half * samples, transcendentals=0
        ),
        name="prepare",
    )(where, in_hbm(own_pred), rem_pred, in_hbm(noise), in_hbm(observed.reshape(1, -1)),
      in_hbm(noise_var.reshape(1, -1)))


def sum_kernel(keep, *rest):
    *got, total, rounded = rest
    value = keep[...]
    for piece in got:
        value = value + piece[...].astype(F32)
    total[...] = value
    rounded[...] = value.astype(BF16)


def add_up(keep, got):
    return pl.pallas_call(
        sum_kernel,
        in_specs=[pl.BlockSpec(memory_space=pltpu.VMEM)] * (1 + len(got)),
        out_specs=[pl.BlockSpec(memory_space=pltpu.VMEM)] * 2,
        out_shape=[pltpu.VMEM(keep.shape, F32), pltpu.VMEM(keep.shape, BF16)],
        compiler_params=pltpu.CompilerParams(vmem_limit_bytes=SUM_VMEM),
        name="add_up",
    )(keep, *got)


def exchange(value, distance):
    count = lax.axis_size("tile")
    return lax.ppermute(value, "tile", [(i, i ^ distance) for i in range(count)])


def swap_group(value):
    return lax.ppermute(value, "mem", [(0, 1), (1, 0)])


def tile_kernel(half, tiles, chunk, where, anom, base, scale, *rest):
    outs = rest[:tiles]
    diag_acc, left_acc, both_acc, inner, outer = rest[tiles:]
    quarter = half // 2
    group = where[0]
    own_at = pl.multiple_of(group * half, half)
    quarter_at = pl.multiple_of(group * quarter, quarter)

    def terms(step):
        here = pl.ds(pl.multiple_of(step * chunk, chunk), chunk)
        own = anom[pl.ds(own_at, half), here]
        quarter_rows = anom[pl.ds(quarter_at, quarter), here]
        forcing = base[:, here]
        for t in range(tiles):
            weight = scale[t:t + 1, here].astype(BF16)
            inner[t * half:(t + 1) * half, :] = own * weight
            outer[t * half:(t + 1) * half, :] = forcing * weight
            at = tiles * half + t * quarter
            outer[at:at + quarter, :] = quarter_rows * weight
        diag = dot_nt(inner[...], own)
        left = dot_nt(outer[0:tiles * half, :], anom[0:half, here])
        both = dot_nt(outer[...], anom[half:2 * half, here])
        return diag, left, both

    diag_acc[...], left_acc[...], both_acc[...] = terms(0)

    @pl.loop(1, anom.shape[1] // chunk)
    def _(step):
        diag, left, both = terms(step)
        diag_acc[...] += diag
        left_acc[...] += left
        both_acc[...] += both

    piece = quarter // 2
    ens_rows = quarter + piece + quarter
    for t, out in enumerate(outs):
        at = tiles * half + t * quarter
        top = t * half
        middle = top + quarter
        own_rows = slice(top, top + half)
        out[0:quarter, 0:quarter] = diag_acc[top:middle, 0:quarter].astype(out.dtype)
        out[0:quarter, quarter:half] = diag_acc[middle:middle + quarter, quarter:half].astype(out.dtype)
        out[quarter:quarter + piece, 0:quarter] = diag_acc[top:top + piece, quarter:half].astype(out.dtype)
        out[quarter:quarter + piece, quarter:half] = diag_acc[top + piece:middle, quarter:half].astype(out.dtype)
        out[quarter + piece:ens_rows, :] = both_acc[at:at + quarter, :].astype(out.dtype)
        out[ens_rows:ens_rows + half, :] = left_acc[own_rows, :].astype(out.dtype)
        out[ens_rows + half:ens_rows + 2 * half, :] = both_acc[own_rows, :].astype(out.dtype)


def tile_terms(where, anom, base, scale, kinds):
    half, samples = base.shape
    tiles = scale.shape[0]
    chunk = min(2048, samples)
    rows = half * 13 // 4
    return pl.pallas_call(
        functools.partial(tile_kernel, half, tiles, chunk),
        in_specs=[pl.BlockSpec(memory_space=pltpu.SMEM)] + [pl.BlockSpec(memory_space=pltpu.VMEM)] * 3,
        out_specs=[pl.BlockSpec(memory_space=pltpu.VMEM)] * tiles,
        out_shape=[pltpu.VMEM((rows, half), kind) for kind in kinds],
        scratch_shapes=[
            pltpu.VMEM((tiles * half, half), F32),
            pltpu.VMEM((tiles * half, half), F32),
            pltpu.VMEM((tiles * half * 3 // 2, half), F32),
            pltpu.VMEM((tiles * half, chunk), BF16),
            pltpu.VMEM((tiles * half * 3 // 2, chunk), BF16),
        ],
        compiler_params=pltpu.CompilerParams(vmem_limit_bytes=TILE_VMEM),
        cost_estimate=pl.CostEstimate(
            flops=7 * half * half * samples * tiles, bytes_accessed=6 * half * samples, transcendentals=0
        ),
        name="tile_terms",
    )(where, anom, base, scale)


def solve_kernel(half, where, *refs):
    own_refs, rem_refs, out = refs[0:4], refs[4:8], refs[8]
    matrix, right, own_diag, rem_diag, own_off, rem_off = refs[9:]
    group = where[0]
    rows = half // 4
    members = 2 * half
    prior = members - 1.0
    for k in range(4):
        digit = jnp.bitwise_xor(where[1], k)
        diag_at = pl.ds(pl.multiple_of(digit * rows, rows), rows)
        off_at = pl.ds(pl.multiple_of(digit * (rows // 2), rows // 2), rows // 2)
        edge = rows * 3 // 2
        for refs_k, diag, off in ((own_refs, own_diag, own_off), (rem_refs, rem_diag, rem_off)):
            diag[diag_at, :] = refs_k[k][0:rows, :].astype(F32)
            off[off_at, :] = refs_k[k][rows:edge, :].astype(F32)
        right[diag_at, 0:half] = own_refs[k][edge:edge + rows, :].astype(F32)
        right[diag_at, half:members] = own_refs[k][edge + rows:edge + 2 * rows, :].astype(F32)
    first = group == 0
    off = jnp.concatenate(
        [jnp.where(first, own_off[...], rem_off[...]), jnp.where(first, rem_off[...], own_off[...])], 0
    )
    row_at = lax.broadcasted_iota(jnp.int32, (half, half), 0)
    col_at = lax.broadcasted_iota(jnp.int32, (half, half), 1)
    eye = jnp.where(row_at == col_at, prior, 0.0)
    matrix[0:half, 0:half] = jnp.where(first, own_diag[...], rem_diag[...]) + eye
    matrix[half:members, half:members] = jnp.where(first, rem_diag[...], own_diag[...]) + eye
    matrix[0:half, half:members] = off
    matrix[half:members, 0:half] = off.T
    right[:, 0:half] += jnp.where(first, eye, 0.0)
    right[:, half:members] += jnp.where(first, 0.0, eye)

    whole = matrix[...]
    row_bound = jnp.max(jnp.sum(jnp.abs(whole), axis=1))
    top = jnp.minimum(row_bound, jnp.sqrt(jnp.sum(whole * whole))) * 1.0001
    factor = 2.0 / (top + prior)
    matrix[...] = whole * factor
    right[...] = right[...] * factor

    def update(spread):
        y = matrix[...]
        y_hi = y.astype(BF16)
        y_lo = (y - y_hi.astype(F32)).astype(BF16)
        c = right[...]
        c_hi = c.astype(BF16)
        c_lo = (c - c_hi.astype(F32)).astype(BF16)
        square = spread * spread
        s = 2.0 / (2.0 - square)
        matrix[...] = s * (2.0 * y - (dot_nn(y_hi, y_hi) + dot_nn(y_hi, y_lo) + dot_nn(y_lo, y_hi)))
        right[...] = s * (2.0 * c - (dot_nn(c_hi, y_hi) + dot_nn(c_hi, y_lo) + dot_nn(c_lo, y_hi)))
        return square / (2.0 - square)

    lax.while_loop(lambda spread: spread > 0.02, update, (top - prior) / (top + prior))
    y = matrix[...]
    y_hi = y.astype(BF16)
    y_lo = (y - y_hi.astype(F32)).astype(BF16)
    c = right[...]
    c_hi = c.astype(BF16)
    c_lo = (c - c_hi.astype(F32)).astype(BF16)
    last = 2.0 * c - (dot_nn(c_hi, y_hi) + dot_nn(c_hi, y_lo) + dot_nn(c_lo, y_hi))
    out[...] = last.astype(BF16)


def solve(where, own, rem):
    half = own[0].shape[1]
    return pl.pallas_call(
        functools.partial(solve_kernel, half),
        in_specs=[pl.BlockSpec(memory_space=pltpu.SMEM)] + [pl.BlockSpec(memory_space=pltpu.VMEM)] * 8,
        out_specs=pl.BlockSpec(memory_space=pltpu.VMEM),
        out_shape=jax.ShapeDtypeStruct((half, 2 * half), BF16),
        scratch_shapes=[
            pltpu.VMEM((2 * half, 2 * half), F32),
            pltpu.VMEM((half, 2 * half), F32),
            pltpu.VMEM((half, half), F32),
            pltpu.VMEM((half, half), F32),
            pltpu.VMEM((half // 2, half), F32),
            pltpu.VMEM((half // 2, half), F32),
        ],
        compiler_params=pltpu.CompilerParams(vmem_limit_bytes=VMEM_LIMIT),
        cost_estimate=pl.CostEstimate(
            flops=700 * half**3, bytes_accessed=16 * half * half, transcendentals=0
        ),
        name="solve",
    )(where, *own, *rem)


def finish_kernel(half, arrivals, where, coeffs, own_sum, rem_sum, own_prod, *rest):
    got = rest[:arrivals]
    own_model, rem_model = rest[arrivals:arrivals + 2]
    out, own_gain, rem_gain = rest[-3:]
    first = where[0] == 0

    @pl.when(pl.program_id(0) == 0)
    def _():
        quarter = half // 2
        piece = quarter // 2
        own = own_sum[...]
        rem = rem_sum[...]

        def diagonal(part):
            side = jnp.concatenate(
                [part[quarter:quarter + piece, 0:quarter], part[quarter:quarter + piece, quarter:half]], 0
            )
            upper = jnp.concatenate([part[0:quarter, 0:quarter], side], 1)
            lower = jnp.concatenate([side.T, part[0:quarter, quarter:half]], 1)
            return jnp.concatenate([upper, lower], 0)

        own_diag = diagonal(own)
        rem_diag = diagonal(rem)
        own_off = own[quarter + piece:]
        rem_off = rem[quarter + piece:]
        top = jnp.where(first, own_diag, rem_diag)
        low = jnp.where(first, rem_diag, own_diag)
        off = jnp.concatenate(
            [jnp.where(first, own_off, rem_off), jnp.where(first, rem_off, own_off)], 0
        )
        left_c = coeffs[:, 0:half]
        right_c = coeffs[:, half:2 * half]
        prod = own_prod[half * 5 // 4:, :]
        for more in got:
            prod = prod + more[half * 5 // 4:, :].astype(F32)
        scale = 1.0 / (2.0 * half - 1.0)
        left = (prod[0:half] - (dot_nn(left_c, top) + dot_nt(right_c, off))) * scale
        right = (prod[half:] - (dot_nn(left_c, off) + dot_nn(right_c, low))) * scale
        mean = (jnp.sum(left, 1, keepdims=True) + jnp.sum(right, 1, keepdims=True)) * (0.5 / half)
        left = (left - mean).astype(BF16)
        right = (right - mean).astype(BF16)
        own_gain[...] = jnp.where(first, left, right)
        rem_gain[...] = jnp.where(first, right, left)

    own = own_model[...]
    update = dot_nn(own_gain[...], own) + dot_nn(rem_gain[...], rem_model[...])
    out[...] = (own.astype(F32) + update).astype(BF16)


def finish(tile, done, where, coeffs, own_sum, rem_sum, own_prod, got, own_model, rem_model):
    half, cells = own_model.shape
    chunk = min(2048, cells // TPD)
    steps = cells // TPD // chunk
    column = lambda j: (0, tile * steps + j)
    whole = lambda j: (0, 0)
    rows = half * 13 // 4
    operands = [where, coeffs, own_sum, rem_sum, own_prod, *got, own_model, rem_model]
    in_specs = (
        [
            pl.BlockSpec(memory_space=pltpu.SMEM),
            pl.BlockSpec((half, 2 * half), whole),
            pl.BlockSpec((half * 5 // 4, half), whole),
            pl.BlockSpec((half * 5 // 4, half), whole),
        ]
        + [pl.BlockSpec((rows, half), whole)] * (1 + len(got))
        + [pl.BlockSpec((half, chunk), column)] * 2
    )
    aliases = {}
    if done is not None:
        aliases = {len(operands): 0}
        operands.append(done)
        in_specs.append(pl.BlockSpec(memory_space=pl.ANY))
    return pl.pallas_call(
        functools.partial(finish_kernel, half, len(got)),
        grid=(steps,),
        in_specs=in_specs,
        out_specs=pl.BlockSpec((half, chunk), column),
        out_shape=jax.ShapeDtypeStruct((half, cells), BF16),
        input_output_aliases=aliases,
        scratch_shapes=[pltpu.VMEM((half, half), BF16)] * 2,
        compiler_params=pltpu.CompilerParams(vmem_limit_bytes=VMEM_LIMIT),
        cost_estimate=pl.CostEstimate(
            flops=4 * half * half * cells // TPD, bytes_accessed=6 * half * cells // TPD, transcendentals=0
        ),
        name="finish",
    )(*operands)


def sample_weights(block_lists, taper_weights, targets, source, inverse_var):
    blocks_local = inverse_var.shape[0] // BLOCK_ROWS
    rows = [lax.dynamic_slice_in_dim(block_lists, target * TPD, TPD, 0) for target in targets]
    tapers = [lax.dynamic_slice_in_dim(taper_weights, target * TPD, TPD, 0) for target in targets]
    rows, tapers = jnp.concatenate(rows, 0), jnp.concatenate(tapers, 0)
    ids = source * blocks_local + jnp.arange(blocks_local, dtype=jnp.int32)
    matches = rows[:, None, :] == ids[None, :, None]
    weights = jnp.sum(jnp.where(matches, tapers[:, None, :], 0.0), axis=2)
    scaled = weights[:, :, None] * inverse_var.reshape(1, blocks_local, BLOCK_ROWS)
    return scaled.reshape(rows.shape[0], -1)


def shards(ensemble, predicted, obs_noise, observed, noise_var, block_lists, taper_weights):
    half = predicted.shape[0]
    count = lax.axis_size("tile")
    index = lax.axis_index("tile")
    where = jnp.stack([lax.axis_index("mem"), index % 4]).astype(jnp.int32)
    rem_pred = swap_group(predicted)

    reach = max(1, count // 16)
    pair = [(i, i ^ 1) for i in range(count)]
    if reach == 1:
        side = 1 - 2 * (index % 2)
        offsets = [-side, side, 0]
    else:
        offsets = [o for o in range(-reach, reach + 1) if o != 0] + [0]
    targets = [(index + o) % count for o in offsets]
    scales = sample_weights(block_lists, taper_weights, targets, index, 1.0 / noise_var)
    scales = [scales[n * TPD:(n + 1) * TPD] for n in range(len(targets))]

    anom, base, keep, *send = prepare(where, predicted, rem_pred, obs_noise, observed, noise_var)
    terms = functools.partial(tile_terms, where, anom, base)
    send, model = lax.optimization_barrier((send, ensemble))
    rem_model = swap_group(model)

    got = [exchange(send[k - 1], k) for k in (1, 2, 3)]
    if reach == 1:
        far, near = scales[0], scales[1]
        far_first, near_second = terms(jnp.concatenate([far[0:1], near[1:2]], 0), (BF16, BF16))
        got, far_first, near_second = lax.optimization_barrier((got, far_first, near_second))
        hop = [(i, (i + 2) % count if i % 2 else (i - 2) % count) for i in range(count)]
        passed = lax.ppermute(far_first, "tile", hop)
        beside = lax.ppermute(near_second, "tile", pair)
    keep, packed = add_up(keep, got)
    bit = 4
    while 2 * bit < count:
        keep, packed = add_up(keep, [exchange(packed, bit)])
        bit *= 2
    if reach == 1:
        packed, mixed = lax.optimization_barrier((packed, jnp.concatenate([near[0:1], far[1:2]], 0)))
    got = exchange(packed, bit)
    if reach == 1:
        near_first, far_second = terms(mixed, (F32, BF16))
        got, near_first, far_second, passed = lax.optimization_barrier((got, near_first, far_second, passed))
        summed = (near_first + passed.astype(F32)).astype(BF16)
    _, packed = add_up(keep, [got])
    packed, scales[-1] = lax.optimization_barrier((packed, scales[-1]))
    own = [packed] + [exchange(packed, k) for k in (1, 2, 3)]
    own_terms = terms(scales[-1], (F32,) * TPD)
    if reach == 1:
        if ACROSS_EARLY:
            across = lax.ppermute(summed, "tile", pair)
            own, own_terms, beside, far_second, across = lax.optimization_barrier(
                (own, own_terms, beside, far_second, across))
        else:
            own, own_terms, beside, far_second, summed = lax.optimization_barrier(
                (own, own_terms, beside, far_second, summed))
            across = lax.ppermute(summed, "tile", pair)
        away = [(i, (i + 2 * (i % 2) - 1) % count) for i in range(count)]
        arrivals = [[across], [beside, lax.ppermute(far_second, "tile", away)]]
    else:
        arrivals = [[] for _ in range(TPD)]
        for offset, scale in zip(offsets[:-1], scales):
            hop = [(i, (i + offset) % count) for i in range(count)]
            for pieces, piece in zip(arrivals, terms(scale, (BF16,) * TPD)):
                pieces.append(lax.ppermute(piece, "tile", hop))
    rem = [swap_group(piece) for piece in own]
    sums = []
    for t in range(TPD):
        if t == TPD - 1:
            coeffs = solve(where, own, rem)
            coeffs, arrivals[t] = lax.optimization_barrier((coeffs, arrivals[t]))
        own_sum = own_terms[t][:half * 5 // 4]
        for piece in arrivals[t]:
            own_sum = own_sum + piece[:half * 5 // 4].astype(F32)
        own_sum = own_sum.astype(BF16)
        sums.append((own_sum, swap_group(own_sum)))
    done = None
    for t in range(TPD):
        done = finish(t, done, where, coeffs, *sums[t], own_terms[t], arrivals[t], ensemble, rem_model)
    return done


def solution(mesh):
    in_specs = (
        P("mem", "tile"),
        P("mem", "tile"),
        P("mem", "tile"),
        P("tile"),
        P("tile"),
        P(),
        P(),
    )
    out_specs = P("mem", "tile")
    return jax.shard_map(shards, mesh=mesh, in_specs=in_specs, out_specs=out_specs, check_vma=False)
```
